32 devices in a mesh: shot: 2 (over core), probe: 16 (over z, y, x).
Axes of the slice: x: 2, y: 2, z: 4, core: 2. Of those that a mesh axis runs over, the one named last changes fastest.
Arguments:
- probes: float32 [32, 256, 512], P('probe'), may hold values from -6 to 6
- coarse_sample: float32 [32, 256, 512], P('probe', 'shot'), may hold values from -6 to 6
- coefficient: float32 [256, 512], replicated, may hold values from 0.05 to 0.45
- receiver: float32 [256, 512], replicated, may hold values from 0.05 to 0.5
- checkpoints: float32 [4, 2, 256, 512], P('shot', None, 'probe'), may hold values from -6 to 6
- encodings: int32 [4, 256], P('shot'), may hold values from -1 to 1, as said below
- wavelet: float32 [3, 256], replicated, may hold values from -6 to 6
- bounds: int32 [33], replicated, may hold values from 0 to 256, as said below
Outputs:
- samples: float32 [32, 256, 512], P('probe', 'shot')
The draws below stay inside these ranges and needn't reach their ends.
Inputs may be any that keep to these rules, and one draw needn't show every extreme that they name: `encodings`: every entry is -1 or 1. bounds[0] = 0 and bounds[32] = 256; the entries rise strictly; blocks 2 i and 2 i + 1 together hold exactly 16 rows.
All inputs are finite; a program needn't handle non-finite values.
Results may differ from the reference program's by a relative error of at most 0.000094.
Values sent between devices are 32-bit elements; how exact they have to be, the bound alone decides.
A program may use at most 128 MiB of HBM per device.

```python
import math
import jax
import jax.numpy as jnp
from jax import lax

NZ = 512
NSHOT = 256
NT = 4
BLK = 8
NX = 256
SUPER = 4
PROBES = 32
NB = 32


def draw_encodings(key, part):
    signs = jax.random.randint(key, (SUPER, NSHOT), 0, 2)
    return (signs * 2 - 1).astype(jnp.int32)


def draw_bounds(key, part):
    half = BLK // 2
    offset = jax.random.randint(key, (NB // 2,), 1 - half, half)
    sizes = jnp.stack([BLK + offset, BLK - offset], axis=1).reshape(-1)
    return jnp.concatenate([jnp.zeros((1,), jnp.int32), jnp.cumsum(sizes).astype(jnp.int32)])


def block_scale(rng, extent, pieces, smallest, high):
    def one(dim, parts):
        steps = jax.random.uniform(jax.random.fold_in(jax.random.fold_in(rng, 6), dim), (parts,), jnp.float32, smallest / len(pieces), high / len(pieces))
        return jnp.repeat(jnp.exp(steps), extent[dim] // parts).reshape((-1,) + (1,) * (len(extent) - dim - 1))

    factor_of = one(*pieces[0])
    for cut in pieces[1:]:
        factor_of = factor_of * one(*cut)
    return factor_of


def gaussian(key, dims, spread, limit, shards=(), held_as=jnp.bfloat16):
    result = spread * jax.random.normal(key, dims, jnp.float32)
    if shards:
        result = result * block_scale(key, dims, shards, -0.22, 0.18)
    return jnp.clip(result, -limit, limit).astype(held_as)


def setup_inputs(seed: int = 0) -> dict:
    streams_of = jax.random.split(jax.random.key(seed), 9)
    return {
        "probes": gaussian(streams_of[0], (PROBES, NX, NZ), 1.0, 6.0, ((0, 16),), jnp.float32),
        "coarse_sample": gaussian(streams_of[1], (PROBES, NX, NZ), 1.0, 6.0, ((0, 16), (1, 2)), jnp.float32),
        "coefficient": jnp.clip(jnp.exp(jax.random.uniform(streams_of[2], (NX, NZ), jnp.float32, math.log(0.05), math.log(0.45))), 0.05, 0.45),
        "receiver": jnp.clip(jnp.exp(jax.random.uniform(streams_of[3], (NX, NZ), jnp.float32, math.log(0.05), math.log(0.5))), 0.05, 0.5),
        "checkpoints": gaussian(streams_of[4], (SUPER, 2, NX, NZ), 1.0, 6.0, ((0, 2), (2, 16)), jnp.float32),
        "encodings": draw_encodings(jax.random.fold_in(streams_of[8], 71), 0),
        "wavelet": gaussian(streams_of[6], (NT - 1, NSHOT), 1.0, 6.0, (), jnp.float32),
        "bounds": draw_bounds(jax.random.fold_in(streams_of[8], 71), 0),
    }


def laplace(values):
    pad_width = [(0, 0)] * (values.ndim - 2) + [(1, 1), (1, 1)]
    padded = jnp.pad(values, pad_width)
    return padded[..., 2:, 1:-1] + padded[..., :-2, 1:-1] + padded[..., 1:-1, 2:] + padded[..., 1:-1, :-2] - 4.0 * values

def shot_sources(encodings, wavelet):
    columns = jnp.arange(NZ)
    spacing = NZ // NSHOT
    position = jnp.arange(NSHOT) * NZ // NSHOT + spacing // 2
    onehot = (position[:, None] == columns[None, :]).astype(jnp.float32)
    amplitude = encodings.astype(jnp.float32)[:, None, :] * wavelet[None, :, :]
    return jnp.einsum('stk,kz->stz', amplitude, onehot, precision=lax.Precision.HIGHEST)

def block_parity(row_index, bounds):
    inner = bounds[1:-1]
    return lax.optimization_barrier(jnp.sum((row_index[:, None] >= inner[None, :]).astype(jnp.int32), axis=1)) % 2

def forward_levels(pair, source_rows, coefficient):
    at_source = (jnp.arange(NX) == NX // 2).astype(jnp.float32)[:, None]
    before = pair[0]
    current = pair[1]
    history = [current]
    for moment in range(NT - 1):
        following = 2.0 * current - before + coefficient * laplace(current) + at_source * source_rows[moment][None, :]
        before, current = (current, following)
        history.append(current)
    return jnp.stack(history)

def increments(vectors, levels, coefficient, receiver):
    before = jnp.zeros_like(vectors)
    current = jnp.zeros_like(vectors)
    observed = []
    for moment in range(NT):
        following = 2.0 * current - before + coefficient * laplace(current) + vectors * levels[moment]
        before, current = (current, following)
        observed.append(receiver * following)
    return jnp.stack(observed)

def reference(probes, coarse_sample, coefficient, receiver, checkpoints, encodings, wavelet, bounds):
    parity = block_parity(jnp.arange(NX), bounds)
    colour = jnp.arange(PROBES) % 2
    support = (parity[None, :] == colour[:, None]).astype(jnp.float32)
    vectors = probes * support[:, :, None]
    sources = shot_sources(encodings, wavelet)

    def one_shot(accumulated, inputs):
        pair, source_rows = inputs
        levels = forward_levels(pair, source_rows, coefficient)

        def observe(moved):
            return increments(moved, levels, coefficient, receiver)
        observed, pullback = jax.vjp(observe, vectors)
        gradient, = pullback(observed)
        return (accumulated + gradient, None)
    hessian, _ = lax.scan(one_shot, jnp.zeros_like(vectors), (checkpoints, sources))
    keep = (parity[None, :] != colour[:, None]).astype(jnp.float32)
    return keep[:, :, None] * (hessian - coarse_sample)
```

```python
import functools

import jax
import jax.numpy as jnp
from jax import lax
from jax.experimental import pallas as pl
from jax.experimental.pallas import tpu as pltpu
from jax.sharding import PartitionSpec as P

MESH = pl.DeviceIdType.MESH
SUB = 8
LANE = 128
INNER = 4
UNROLL = 4


def kernel(
    num_shot_devices,
    num_probe_devices,
    bounds_ref,
    encodings_ref,
    wavelet_ref,
    probes_hbm,
    coarse_hbm,
    coefficient_hbm,
    receiver_hbm,
    checkpoints_hbm,
    out_hbm,
    own_in,
    own,
    probes_in,
    coarse_in,
    coefficient_in,
    receiver_in,
    inverse,
    spread_table,
    collect_table,
    parity_in,
    parity_out,
    coef,
    centre,
    weight,
    vec,
    um,
    u0,
    u1,
    u2,
    u3,
    d1,
    d2,
    d3,
    e4,
    e3,
    e2,
    total,
    packed,
    partial,
    result_out,
    source,
    load_sem,
    own_sem,
    recv_sem,
    send_sem,
    line_sem,
    pack_sem,
    out_sem,
    swap_send,
    swap_recv,
):
    members, levels, chunk, width = checkpoints_hbm.shape
    num_probes, num_rows, _ = probes_hbm.shape
    out_rows = coarse_hbm.shape[1]
    tiles = num_rows // SUB
    groups = width // LANE
    cols = [pl.ds(c * LANE, LANE) for c in range(groups)]
    steps = wavelet_ref.shape[0]
    line = num_probe_devices // INNER
    flags = num_probe_devices * 2
    share = SUB // num_shot_devices
    part_tiles = tiles // num_shot_devices
    block = min(8, part_tiles)
    rows_of_block = block * SUB

    shot = lax.axis_index("shot")
    mine = lax.axis_index("probe")
    z = mine // INNER
    a = mine % INNER
    high, low = a // 2, a % 2
    right = 2 * low + (1 - high)
    left = 2 * (1 - low) + high

    places = {"a": a, "right": right, "left": left, "far": 3 - a}
    ids = {
        (dz, name): (z + dz) * INNER + place
        for dz in range(1 - line, line)
        for name, place in places.items()
    }
    exists = {dz: (z + dz >= 0) & (z + dz < line) for dz in range(1 - line, line)}
    def slot(m, src, t):
        first = src * chunk
        sub = first // tiles
        tile = first % tiles
        if t:
            return u0.at[m, pl.ds(tile + 1, chunk), sub, :]
        return um.at[m, pl.ds(tile, chunk), sub, :]

    def own_copy(m, t):
        return pltpu.make_async_copy(own.at[m, t], slot(m, mine, t), own_sem.at[m * 2 + t])

    load_own = pltpu.make_async_copy(checkpoints_hbm, own_in, load_sem.at[0])
    load_own.start()

    def strided_load(src, dst, base):
        return [
            pltpu.make_async_copy(src.at[pl.ds(k * tiles, tiles), :], dst.at[:, k, :], load_sem.at[base + k])
            for k in range(SUB)
        ]

    load_probes = [
        copy
        for p in range(num_probes)
        for copy in strided_load(probes_hbm.at[p], probes_in.at[p], 1 + p * SUB)
    ]
    base = 1 + num_probes * SUB
    load_coefficient = strided_load(coefficient_hbm, coefficient_in, base)
    load_receiver = strided_load(receiver_hbm, receiver_in, base + SUB)
    base = base + 2 * SUB
    load_out = []
    for k in range(num_shot_devices):
        for e in range(share):
            first = pl.multiple_of(e * tiles + k * part_tiles, SUB)
            near = pl.multiple_of(shot * out_rows + e * tiles + k * part_tiles, SUB)
            load_out.append(
                pltpu.make_async_copy(
                    coefficient_hbm.at[pl.ds(near, part_tiles), :],
                    inverse.at[:, k * share + e, :],
                    load_sem.at[base],
                )
            )
            base += 1
            for p in range(num_probes):
                load_out.append(
                    pltpu.make_async_copy(
                        coarse_hbm.at[p, pl.ds(first, part_tiles), :],
                        coarse_in.at[p, :, k * share + e, :],
                        load_sem.at[base],
                    )
                )
                base += 1
    for load in load_probes + load_coefficient + load_receiver + load_out:
        load.start()

    barrier = pltpu.get_barrier_semaphore()

    def greet(device):
        pl.semaphore_signal(barrier, inc=1, device_id=device, device_id_type=MESH)

    greet({"probe": ids[0, "right"]})
    greet({"probe": ids[0, "left"]})

    for dz in range(1 - line, line):
        if dz:

            @pl.when(exists[dz])
            def _(dz=dz):
                greet({"probe": ids[dz, "a"]})

    for away in range(1, num_shot_devices):
        greet({"shot": (shot + away) % num_shot_devices})

    def build_tables():
        def body(b, carry):
            rows = pl.ds(pl.multiple_of(b * LANE, LANE), LANE)
            row = lax.broadcasted_iota(jnp.int32, (LANE, width), 0) + b * LANE
            col = lax.broadcasted_iota(jnp.int32, (LANE, width), 1)
            place = groups * (col % LANE) + col // LANE
            spread_table[rows, :] = jnp.where(row == place, 1.0, 0.0).astype(jnp.bfloat16)
            place = groups * (row % LANE) + row // LANE
            collect_table[rows, :] = jnp.where(col == place, 1.0, 0.0).astype(jnp.bfloat16)
            return carry

        lax.fori_loop(0, groups, body, 0)

    def shuffle(x, table):
        high = x.astype(jnp.bfloat16)
        rest = x - high.astype(jnp.float32)
        middle = rest.astype(jnp.bfloat16)
        low = (rest - middle.astype(jnp.float32)).astype(jnp.bfloat16)
        moved = [
            jnp.dot(piece, table[...], preferred_element_type=jnp.float32)
            for piece in (high, middle, low)
        ]
        return moved[0] + (moved[1] + moved[2])

    build_tables()
    load_own.wait()
    count = members * levels * chunk
    own[...] = shuffle(own_in[...].reshape(count, width), spread_table).reshape(own.shape)
    pl.semaphore_wait(barrier, line - 1 + 2 + num_shot_devices - 1)

    sent = []

    def send(m, src, t, target, sem, cond=None):
        def copy():
            return pltpu.make_async_remote_copy(
                src_ref=own.at[m, t] if src == (0, "a") else slot(m, ids[src], t),
                dst_ref=slot(m, ids[src], t),
                send_sem=sem(),
                recv_sem=recv_sem.at[m * flags + ids[src] * 2 + t],
                device_id={"probe": ids[target]},
                device_id_type=MESH,
            )

        copy().start()
        sent.append((copy, cond))

    def arrive(m, src, t):
        pltpu.make_async_remote_copy(
            src_ref=slot(m, ids[src], t),
            dst_ref=slot(m, ids[src], t),
            send_sem=send_sem.at[m * flags + ids[src] * 2 + t],
            recv_sem=recv_sem.at[m * flags + ids[src] * 2 + t],
            device_id={"probe": ids[0, "right"]},
            device_id_type=MESH,
        ).wait_recv()

    def ring(m, src, t, name, cond=None):
        lane = 0 if name == "right" else 1
        send(
            m,
            src,
            t,
            (0, name),
            lambda: send_sem.at[(lane * members + m) * flags + ids[src] * 2 + t],
            cond,
        )

    def spread(m, src, cond=None):
        for t in (0, 1):
            ring(m, src, t, "right", cond)
            ring(m, src, 1 - t, "left", cond)

    def begin(m):
        for t in range(2):
            own_copy(m, t).start()
        for k in range(1, line):
            for dz in (k, -k):

                @pl.when(exists[dz])
                def _(dz=dz):
                    for t in (0, 1):
                        index = ((dz + line - 1) * members + m) * 2 + t
                        send(m, (0, "a"), t, (dz, "a"), lambda index=index: line_sem.at[index], exists[dz])

        spread(m, (0, "a"))

    def column(m, k):
        for dz, here in sides(k):

            @pl.when(here)
            def _(dz=dz, here=here):
                for t in (0, 1):
                    arrive(m, (dz, "a"), t)
                spread(m, (dz, "a"), here)

    def sides(k):
        if k == 0:
            return ((0, None),)
        return ((-k, exists[-k]), (k, exists[k]))

    def guarded(cond, fun):
        if cond is None:
            fun()
        else:
            pl.when(cond)(fun)

    def relay(m, k):
        for dz, cond in sides(k):

            def run(dz=dz, cond=cond):
                arrive(m, (dz, "left"), 0)
                ring(m, (dz, "left"), 0, "right", cond)
                arrive(m, (dz, "right"), 1)
                ring(m, (dz, "right"), 1, "left", cond)

            guarded(cond, run)

    def finish(m, k):
        for dz, cond in sides(k):

            def run(dz=dz):
                arrive(m, (dz, "left"), 1)
                arrive(m, (dz, "right"), 0)
                arrive(m, (dz, "far"), 0)
                arrive(m, (dz, "far"), 1)

            guarded(cond, run)

    def gather_steps(m):
        plan = []
        for k in range(1, line):
            plan.append(lambda k=k: column(m, k))
        for k in range(line):
            plan.append(lambda k=k: relay(m, k))
        return plan

    def gather_end(m):
        for k in range(line):
            finish(m, k)
        for t in range(2):
            own_copy(m, t).wait()

    for m in range(members):
        begin(m)

    row_in_tile = lax.broadcasted_iota(jnp.int32, (SUB, LANE), 0)
    lane_index = lax.broadcasted_iota(jnp.int32, (SUB, LANE), 1)
    at_first = lane_index == 0
    at_last = lane_index == LANE - 1

    def parity_of(rows):
        count = jnp.zeros((SUB, LANE), jnp.int32)
        for b in range(1, bounds_ref.shape[0] - 1):
            count = count + jnp.where(rows >= bounds_ref[b], 1, 0)
        return count % 2

    def prepare_sources():
        shots = wavelet_ref.shape[1]
        spacing = width // shots
        k = lax.broadcasted_iota(jnp.int32, (shots, width), 0)
        position = k * width // shots + spacing // 2
        index = lax.broadcasted_iota(jnp.int32, (shots, width), 1)
        onehot = jnp.where(position == groups * (index % LANE) + index // LANE, 1.0, 0.0)
        for m in range(members):
            amplitude = encodings_ref[m : m + 1, :].astype(jnp.float32) * wavelet_ref[...]
            source[m, 0:steps, :] = jnp.dot(
                amplitude,
                onehot,
                precision=lax.Precision.HIGHEST,
                preferred_element_type=jnp.float32,
            )

    def by_block(first, last, run):
        def body(b, carry):
            run(pl.multiple_of(b * block, block))
            return carry

        lax.fori_loop(first, last, body, 0)

    def flat(x):
        return x.reshape(rows_of_block, width)

    def tiled(x):
        return x.reshape(block, SUB, width)

    def prepare_coefficient(j):
        at = pl.ds(j, block)
        value = tiled(shuffle(flat(coefficient_in[at]), spread_table))
        coef[at] = value
        centre[at] = 2.0 - 4.0 * value

    def prepare_weight(j):
        at = pl.ds(j, block)
        seen = tiled(shuffle(flat(receiver_in[at]), spread_table))
        weight[at] = coef[at] * (seen * seen)

    def prepare_vectors(j):
        at = pl.ds(j, block)
        rows = []
        for i in range(block):
            parity = parity_of(row_in_tile * tiles + (j + i))
            parity_in[j + i] = parity
            rows.append(
                jnp.concatenate(
                    [
                        jnp.where(parity == 0, probes_in[0, j + i, :, c], probes_in[1, j + i, :, c])
                        for c in cols
                    ],
                    axis=1,
                )
            )
        both = tiled(shuffle(jnp.concatenate(rows, axis=0), spread_table))
        vec[2, at] = both
        for i in range(block):
            even = parity_in[j + i] == 0
            for c in cols:
                value = vec[2, j + i, :, c]
                vec[0, j + i, :, c] = jnp.where(even, value, 0.0)
                vec[1, j + i, :, c] = jnp.where(even, 0.0, value)

    def prepare_out():
        def body(i, carry):
            row = shot * out_rows + (row_in_tile % share) * tiles + (row_in_tile // share) * part_tiles + i
            parity_out[i] = parity_of(row)
            for c in cols:
                inverse[i, :, c] = 1.0 / inverse[i, :, c]
            return carry

        lax.fori_loop(0, part_tiles, body, 0)

    def halo(field):
        for c in cols:
            above = pltpu.roll(field[tiles, :, c], 1, 0)
            field[0, :, c] = jnp.where(row_in_tile == 0, 0.0, above)
            below = pltpu.roll(field[1, :, c], SUB - 1, 0)
            field[tiles + 1, :, c] = jnp.where(row_in_tile == SUB - 1, 0.0, below)

    def advance(field, before, j):
        here = [field[j + 1, :, c] for c in cols]
        west = [jnp.where(at_first, 0.0, pltpu.roll(here[-1], 1, 1))] + here[:-1]
        east = here[1:] + [jnp.where(at_last, 0.0, pltpu.roll(here[0], LANE - 1, 1))]
        moved = []
        for i, c in enumerate(cols):
            near = (field[j, :, c] + field[j + 2, :, c]) + (west[i] + east[i])
            value = centre[j, :, c] * here[i] + coef[j, :, c] * near
            if before is not None:
                value = value - before(j, c)
            moved.append(value)
        return moved

    def inner(field):
        return lambda j, c: field[j + 1, :, c]

    def sweep(body):
        def run(j, carry):
            body(j)
            return carry

        lax.fori_loop(0, tiles, run, 0, unroll=UNROLL)

    pair = range(num_probes)

    def start_fields(m):
        def body(j):
            for c in cols:
                value = u0[m, j + 1, :, c]
                for p in pair:
                    d1[p, j + 1, :, c] = vec[p, j, :, c] * value

        sweep(body)
        halo(u0.at[m])
        for p in pair:
            halo(d1.at[p])

    def levels_step(m, t):
        field = (u0.at[m], u1, u2)[t]
        before = (lambda j, c: um[m, j, :, c], inner(u0.at[m]), inner(u1))[t]
        result = (u1, u2, u3)[t]

        def body(j):
            for c, value in zip(cols, advance(field, before, j)):
                result[j + 1, :, c] = value

        sweep(body)
        for c in cols:
            row = jnp.broadcast_to(source[m, t : t + 1, c], (SUB, LANE))
            result[1, :, c] = result[1, :, c] + jnp.where(row_in_tile == SUB // 2, row, 0.0)
        if t < 2:
            halo(result)

    def chosen(j, values, i):
        return jnp.where(parity_in[j] == 1, values[0][i], values[1][i])

    def forward(m, t):
        level = (u1, u2, u3)[t]
        delta = (d1, d2, d3)[t]
        delta_before = (None, d1, d2)[t]
        delta_next = (d2, d3, e4)[t]

        def body(j):
            values = []
            for p in pair:
                prior = None if delta_before is None else inner(delta_before.at[p])
                step = advance(delta.at[p], prior, j)
                for i, c in enumerate(cols):
                    step[i] = step[i] + vec[p, j, :, c] * level[j + 1, :, c]
                    if t == 2:
                        step[i] = weight[j, :, c] * step[i]
                    delta_next[p, j + 1, :, c] = step[i]
                values.append(step)
            if t == 2:
                for i, c in enumerate(cols):
                    gain = level[j + 1, :, c] * chosen(j, values, i)
                    if m:
                        gain = total[j, :, c] + gain
                    total[j, :, c] = gain

        sweep(body)
        for p in pair:
            halo(delta_next.at[p])

    def adjoint(m, t):
        field = (e4, e3, e2)[t]
        before = (None, e4, e3)[t]
        result = (e3, e2, None)[t]
        delta = (d3, d2, d1)[t]
        level = (u2, u1, u0.at[m])[t]

        def body(j):
            values = []
            for p in pair:
                prior = None if before is None else inner(before.at[p])
                step = advance(field.at[p], prior, j)
                for i, c in enumerate(cols):
                    step[i] = step[i] + weight[j, :, c] * delta[p, j + 1, :, c]
                    if result is not None:
                        result[p, j + 1, :, c] = step[i]
                values.append(step)
            for i, c in enumerate(cols):
                total[j, :, c] = total[j, :, c] + level[j + 1, :, c] * chosen(j, values, i)

        sweep(body)
        if result is not None:
            for p in pair:
                halo(result.at[p])

    def piece(k, device):
        first = pl.multiple_of(device * share, share)
        return total.at[pl.ds(k * part_tiles, part_tiles), pl.ds(first, share), :]

    def pack():
        return [
            pltpu.make_async_copy(piece(k, shot), packed.at[:, pl.ds(k * share, share), :], pack_sem.at[k])
            for k in range(num_shot_devices)
        ]

    def swap():
        copies = []
        for away in range(1, num_shot_devices):
            other = (shot + away) % num_shot_devices
            for k in range(num_shot_devices):
                copies.append(
                    pltpu.make_async_remote_copy(
                        src_ref=piece(k, other),
                        dst_ref=partial.at[away - 1, :, pl.ds(k * share, share), :],
                        send_sem=swap_send.at[away - 1, k],
                        recv_sem=swap_recv.at[away - 1, k],
                        device_id={"shot": other},
                        device_id_type=MESH,
                    )
                )
        return copies

    def combine(j):
        at = pl.ds(j, block)
        value = packed[at]
        for away in range(1, num_shot_devices):
            value = value + partial[away - 1, at]
        value = tiled(shuffle(flat(value), collect_table)) * inverse[at]
        for p in pair:
            for i in range(block):
                keep = parity_out[j + i] != p % 2
                for n, c in enumerate(cols):
                    piece_of = value[i, :, n * LANE : (n + 1) * LANE] - coarse_in[p, j + i, :, c]
                    result_out[p, j + i, :, c] = jnp.where(keep, piece_of, 0.0)

    def deliver():
        copies = []
        for p in pair:
            for k in range(num_shot_devices):
                for e in range(share):
                    copies.append(
                        pltpu.make_async_copy(
                            result_out.at[p, :, k * share + e, :],
                            out_hbm.at[p, pl.ds(e * tiles + k * part_tiles, part_tiles), :],
                            out_sem.at[(p * num_shot_devices + k) * share + e],
                        )
                    )
        return copies

    blocks = tiles // block
    half = blocks // 2
    work = []

    def vectors_work():
        for load in load_probes:
            load.wait()
        by_block(0, blocks, prepare_vectors)

    def coefficient_work():
        for load in load_coefficient:
            load.wait()
        by_block(0, blocks, prepare_coefficient)

    def weight_work():
        for load in load_receiver:
            load.wait()
        by_block(0, blocks, prepare_weight)

    def out_work():
        for load in load_out:
            load.wait()
        prepare_out()

    work = [prepare_sources, coefficient_work, weight_work, vectors_work, out_work]
    for step in gather_steps(0):
        step()
        if work:
            work.pop(0)()
    for rest in work:
        rest()
    for m in range(members):
        plan = gather_steps(m + 1) if m + 1 < members else []
        if plan:
            for _ in range(line - 1):
                plan.pop(0)()
        gather_end(m)
        stages = [lambda: start_fields(m)]
        stages += [lambda t=t: levels_step(m, t) for t in range(3)]
        stages += [lambda t=t: forward(m, t) for t in range(3)]
        stages += [lambda t=t: adjoint(m, t) for t in range(3)]
        for stage in stages:
            stage()
            if plan:
                plan.pop(0)()
        for step in plan:
            step()
    copies = swap()
    packs = pack()
    for copy in copies + packs:
        copy.start()
    for copy in packs:
        copy.wait()
    for copy in copies:
        copy.wait_recv()
    by_block(0, part_tiles // block, combine)
    outs = deliver()
    for copy in outs:
        copy.start()
    for copy in copies:
        copy.wait_send()
    for copy, cond in sent:
        guarded(cond, lambda copy=copy: copy().wait_send())
    for copy in outs:
        copy.wait()


def on_device(
    num_shot_devices,
    num_probe_devices,
    probes,
    coarse_sample,
    coefficient,
    receiver,
    checkpoints,
    encodings,
    wavelet,
    bounds,
):
    members, levels, chunk, width = checkpoints.shape
    num_probes, num_rows, _ = probes.shape
    out_rows = coarse_sample.shape[1]
    tiles = num_rows // SUB
    line = num_probe_devices // INNER
    f32 = jnp.float32

    share = SUB // num_shot_devices
    part_tiles = tiles // num_shot_devices

    def plain(*lead):
        return pltpu.VMEM((*lead, tiles, SUB, width), f32)

    def ringed(*lead):
        return pltpu.VMEM((*lead, tiles + 2, SUB, width), f32)

    def part(*lead):
        return pltpu.VMEM((*lead, part_tiles, SUB, width), f32)

    others = num_shot_devices - 1
    anywhere = pl.BlockSpec(memory_space=pl.ANY)
    vmem = pl.BlockSpec(memory_space=pltpu.VMEM)
    loads = 1 + (num_probes + 2) * SUB + (1 + num_probes) * SUB
    return pl.pallas_call(
        functools.partial(kernel, num_shot_devices, num_probe_devices),
        out_shape=jax.ShapeDtypeStruct(coarse_sample.shape, f32),
        in_specs=[pl.BlockSpec(memory_space=pltpu.SMEM), vmem, vmem] + [anywhere] * 5,
        out_specs=anywhere,
        scratch_shapes=[
            pltpu.VMEM(checkpoints.shape, f32),
            pltpu.VMEM(checkpoints.shape, f32),
            plain(num_probes),
            part(num_probes),
            plain(),
            plain(),
            part(),
            pltpu.VMEM((width, width), jnp.bfloat16),
            pltpu.VMEM((width, width), jnp.bfloat16),
            pltpu.VMEM((tiles, SUB, LANE), jnp.int32),
            pltpu.VMEM((part_tiles, SUB, LANE), jnp.int32),
            plain(),
            plain(),
            plain(),
            plain(num_probes + 1),
            plain(members),
            ringed(members),
            ringed(),
            ringed(),
            ringed(),
            ringed(num_probes),
            ringed(num_probes),
            ringed(num_probes),
            ringed(num_probes),
            ringed(num_probes),
            ringed(num_probes),
            plain(),
            part(),
            part(others),
            part(num_probes),
            pltpu.VMEM((members, SUB, width), f32),
            pltpu.SemaphoreType.DMA((loads,)),
            pltpu.SemaphoreType.DMA((members * levels,)),
            pltpu.SemaphoreType.DMA((members * num_probe_devices * levels,)),
            pltpu.SemaphoreType.DMA((2 * members * num_probe_devices * levels,)),
            pltpu.SemaphoreType.DMA(((2 * line - 1) * members * levels,)),
            pltpu.SemaphoreType.DMA((num_shot_devices,)),
            pltpu.SemaphoreType.DMA((num_probes * SUB,)),
            pltpu.SemaphoreType.DMA((others, num_shot_devices)),
            pltpu.SemaphoreType.DMA((others, num_shot_devices)),
        ],
        compiler_params=pltpu.CompilerParams(
            collective_id=0, has_side_effects=True, vmem_limit_bytes=60 * 1024 * 1024
        ),
    )(
        bounds,
        encodings,
        wavelet,
        probes,
        coarse_sample,
        coefficient,
        receiver,
        checkpoints,
    )


def solution(mesh):
    return jax.shard_map(
        functools.partial(on_device, mesh.shape["shot"], mesh.shape["probe"]),
        mesh=mesh,
        in_specs=(
            P("probe", None, None),
            P("probe", "shot", None),
            P(),
            P(),
            P("shot", None, "probe", None),
            P("shot", None),
            P(),
            P(),
        ),
        out_specs=P("probe", "shot", None),
        check_vma=False,
    )
```

```python
import functools

import jax
import jax.numpy as jnp
from jax import lax
from jax.experimental import pallas as pl
from jax.experimental.pallas import tpu as pltpu
from jax.sharding import PartitionSpec as P

MESH = pl.DeviceIdType.MESH
SUB = 8
LANE = 128
INNER = 4
UNROLL = 16
BY_LINE = ()


def kernel(
    num_shot_devices,
    num_probe_devices,
    bounds_ref,
    encodings_ref,
    wavelet_ref,
    probes_hbm,
    coarse_hbm,
    coefficient_hbm,
    receiver_hbm,
    checkpoints_hbm,
    out_hbm,
    own_in,
    own,
    probes_in,
    coarse_in,
    coefficient_in,
    receiver_in,
    inverse,
    spread_table,
    collect_table,
    parity_in,
    parity_out,
    coef,
    centre,
    weight,
    vec,
    lev,
    counter,
    u1,
    u2,
    u3,
    d1,
    d2,
    d3,
    e4,
    e3,
    e2,
    total,
    packed,
    partial,
    result_out,
    source,
    load_sem,
    own_sem,
    hop_sem,
    far_sem,
    send_sem,
    pack_sem,
    out_sem,
    swap_send,
    swap_recv,
):
    members, levels, chunk, width = checkpoints_hbm.shape
    num_probes, num_rows, _ = probes_hbm.shape
    out_rows = coarse_hbm.shape[1]
    tiles = num_rows // SUB
    groups = width // LANE
    cols = [pl.ds(c * LANE, LANE) for c in range(groups)]
    steps = wavelet_ref.shape[0]
    line = num_probe_devices // INNER
    share = SUB // num_shot_devices
    part_tiles = tiles // num_shot_devices
    block = min(8, part_tiles)
    rows_of_block = block * SUB

    shot = lax.axis_index("shot")
    mine = lax.axis_index("probe")
    z = mine // INNER
    a = mine % INNER
    high, low = a // 2, a % 2
    right = 2 * low + (1 - high)
    left = 2 * (1 - low) + high

    places = {"a": a, "right": right, "left": left, "far": 3 - a}
    ids = {
        (dz, name): (z + dz) * INNER + place
        for dz in range(1 - line, line)
        for name, place in places.items()
    }
    exists = {dz: (z + dz >= 0) & (z + dz < line) for dz in range(1 - line, line)}
    def slot(m, src, t=None):
        first = src * chunk
        rows = pl.ds(first % tiles + 1, chunk)
        if t is None:
            return lev.at[m, :, rows, first // tiles, :]
        return lev.at[m, t, rows, first // tiles, :]

    load_own = pltpu.make_async_copy(checkpoints_hbm, own_in, own_sem.at[0])
    load_own.start()

    barrier = pltpu.get_barrier_semaphore()

    def greet(device):
        pl.semaphore_signal(barrier, inc=1, device_id=device, device_id_type=MESH)

    greet({"probe": ids[0, "right"]})
    greet({"probe": ids[0, "left"]})

    for dz in range(1 - line, line):
        if dz:

            @pl.when(exists[dz])
            def _(dz=dz):
                greet({"probe": ids[dz, "a"]})

    for away in range(1, num_shot_devices):
        greet({"shot": (shot + away) % num_shot_devices})

    def build_table(table, spread):
        def body(b, carry):
            rows = pl.ds(pl.multiple_of(b * LANE, LANE), LANE)
            row = lax.broadcasted_iota(jnp.int32, (LANE, width), 0) + b * LANE
            col = lax.broadcasted_iota(jnp.int32, (LANE, width), 1)
            fine, place = (row, col) if spread else (col, row)
            match = fine == groups * (place % LANE) + place // LANE
            table[rows, :] = jnp.where(match, 1.0, 0.0).astype(jnp.bfloat16)
            return carry

        lax.fori_loop(0, groups, body, 0)

    def shuffle(x, table):
        high = x.astype(jnp.bfloat16)
        rest = x - high.astype(jnp.float32)
        middle = rest.astype(jnp.bfloat16)
        low = (rest - middle.astype(jnp.float32)).astype(jnp.bfloat16)
        moved = [
            jnp.dot(piece, table[...], preferred_element_type=jnp.float32)
            for piece in (high, middle, low)
        ]
        return moved[0] + (moved[1] + moved[2])

    build_table(spread_table, True)
    load_own.wait()
    count = members * levels * chunk
    own[...] = shuffle(own_in[...].reshape(count, width), spread_table).reshape(own.shape)
    pl.semaphore_wait(barrier, line - 1 + 2 + num_shot_devices - 1)

    def send(source, target, place, sem, which=0):
        pltpu.make_async_remote_copy(
            src_ref=source,
            dst_ref=place,
            send_sem=send_sem.at[which],
            recv_sem=sem,
            device_id={"probe": ids[target]},
            device_id_type=MESH,
        ).start()

    def await_bytes(ref, sem):
        pltpu.make_async_copy(ref, ref, sem).wait()

    def guarded(cond, fun):
        if cond is None:
            fun()
        else:
            pl.when(cond)(fun)

    def sides(k):
        if k == 0:
            return ((0, None),)
        return ((-k, exists[-k]), (k, exists[k]))

    def own_to_place(m):
        return pltpu.make_async_copy(own.at[m], slot(m, mine), own_sem.at[1 + m])

    def along_line(m, kind, name, source, dz, ways):
        place = slot(m, ids[dz, name])
        for way in ways:
            pl.when(exists[way])(
                lambda way=way: send(source, (way, "a"), place, hop_sem.at[m, kind, z + dz], 1)
            )

    def to_ring(m, dz):
        source = own.at[m] if dz == 0 else slot(m, ids[dz, "a"])
        place = slot(m, ids[dz, "a"])
        send(source, (0, "right"), place, hop_sem.at[m, 1, z + dz])
        send(source, (0, "left"), place, hop_sem.at[m, 2, z + dz])

    def own_line(m):
        along_line(m, 0, "a", own.at[m], 0, (1, -1))

    def own_ring(m):
        to_ring(m, 0)

    def passing(m, kind, name, k, after):
        for dz, cond in sides(k):

            def run(dz=dz):
                place = slot(m, ids[dz, name])
                await_bytes(place, hop_sem.at[m, kind, z + dz])
                if k == 0:
                    along_line(m, kind, name, place, 0, (1, -1))
                elif k < line - 1:
                    along_line(m, kind, name, place, dz, (1,) if dz < 0 else (-1,))
                after(dz)

            guarded(cond, run)

    def column(m, k):
        passing(m, 0, "a", k, lambda dz: to_ring(m, dz))

    def across(m, k):
        passing(m, 3, "far", k, lambda dz: None)

    def relay(m, k):
        for dz, cond in sides(k):

            def run(dz=dz):
                last = hop_sem.at[m, 3, z] if m in BY_LINE else far_sem.at[m]
                await_bytes(slot(m, ids[dz, "left"]), hop_sem.at[m, 1, z + dz])
                if k == 0 or m not in BY_LINE:
                    place = slot(m, ids[dz, "left"], 0)
                    send(place, (0, "right"), place, last)
                await_bytes(slot(m, ids[dz, "right"]), hop_sem.at[m, 2, z + dz])
                if k == 0 or m not in BY_LINE:
                    place = slot(m, ids[dz, "right"], 1)
                    send(place, (0, "left"), place, last)

            guarded(cond, run)

    def gather_end(m):
        if m not in BY_LINE:
            await_bytes(counter.at[pl.ds(0, line)], far_sem.at[m])
        own_to_place(m).wait()

    def sends_end():
        await_bytes(counter, send_sem.at[0])
        for m in range(members):
            for dz in (1, -1):
                for _ in range(2 if m in BY_LINE else 1):
                    for k in range(line - 1):
                        cond = exists[dz] if k == 0 else exists[dz] & exists[-k * dz]
                        pl.when(cond)(lambda: await_bytes(own.at[0], send_sem.at[1]))

    for m in range(members):
        own_line(m)
    own_ring(0)
    for m in range(members):
        own_to_place(m).start()

    def strided_load(src, dst, sem):
        for k in range(SUB):
            pltpu.make_async_copy(src.at[pl.ds(k * tiles, tiles), :], dst.at[:, k, :], sem).start()

    strided_load(coefficient_hbm, coefficient_in, load_sem.at[0])
    strided_load(receiver_hbm, receiver_in, load_sem.at[1])
    for p in range(num_probes):
        strided_load(probes_hbm.at[p], probes_in.at[p], load_sem.at[2])
    build_table(collect_table, False)
    for k in range(num_shot_devices):
        for e in range(share):
            first = pl.multiple_of(e * tiles + k * part_tiles, SUB)
            near = pl.multiple_of(shot * out_rows + e * tiles + k * part_tiles, SUB)
            pltpu.make_async_copy(
                coefficient_hbm.at[pl.ds(near, part_tiles), :],
                inverse.at[:, k * share + e, :],
                load_sem.at[3],
            ).start()
            for p in range(num_probes):
                pltpu.make_async_copy(
                    coarse_hbm.at[p, pl.ds(first, part_tiles), :],
                    coarse_in.at[p, :, k * share + e, :],
                    load_sem.at[4],
                ).start()

    row_in_tile = lax.broadcasted_iota(jnp.int32, (SUB, LANE), 0)
    lane_index = lax.broadcasted_iota(jnp.int32, (SUB, LANE), 1)
    at_first = lane_index == 0
    at_last = lane_index == LANE - 1

    def parity_of(rows):
        count = jnp.zeros((SUB, LANE), jnp.int32)
        for b in range(1, bounds_ref.shape[0] - 1):
            count = count + jnp.where(rows >= bounds_ref[b], 1, 0)
        return count % 2

    def prepare_sources():
        shots = wavelet_ref.shape[1]
        spacing = width // shots
        k = lax.broadcasted_iota(jnp.int32, (shots, width), 0)
        position = k * width // shots + spacing // 2
        index = lax.broadcasted_iota(jnp.int32, (shots, width), 1)
        onehot = jnp.where(position == groups * (index % LANE) + index // LANE, 1.0, 0.0)
        for m in range(members):
            amplitude = encodings_ref[m : m + 1, :].astype(jnp.float32) * wavelet_ref[...]
            source[m, 0:steps, :] = jnp.dot(
                amplitude,
                onehot,
                precision=lax.Precision.HIGHEST,
                preferred_element_type=jnp.float32,
            )

    def by_block(first, last, run):
        def body(b, carry):
            run(pl.multiple_of(b * block, block))
            return carry

        lax.fori_loop(first, last, body, 0)

    def flat(x):
        return x.reshape(rows_of_block, width)

    def tiled(x):
        return x.reshape(block, SUB, width)

    def prepare_coefficient(j):
        at = pl.ds(j, block)
        value = tiled(shuffle(flat(coefficient_in[at]), spread_table))
        coef[at] = value
        centre[at] = 2.0 - 4.0 * value

    def prepare_weight(j):
        at = pl.ds(j, block)
        seen = tiled(shuffle(flat(receiver_in[at]), spread_table))
        weight[at] = coef[at] * (seen * seen)

    def prepare_vectors(j):
        at = pl.ds(j, block)
        rows = []
        for i in range(block):
            parity = parity_of(row_in_tile * tiles + (j + i))
            parity_in[j + i] = parity
            rows.append(
                jnp.concatenate(
                    [
                        jnp.where(parity == 0, probes_in[0, j + i, :, c], probes_in[1, j + i, :, c])
                        for c in cols
                    ],
                    axis=1,
                )
            )
        both = tiled(shuffle(jnp.concatenate(rows, axis=0), spread_table))
        vec[2, at] = both
        for i in range(block):
            even = parity_in[j + i] == 0
            for c in cols:
                value = vec[2, j + i, :, c]
                vec[0, j + i, :, c] = jnp.where(even, value, 0.0)
                vec[1, j + i, :, c] = jnp.where(even, 0.0, value)

    def prepare_out():
        def body(i, carry):
            row = shot * out_rows + (row_in_tile % share) * tiles + (row_in_tile // share) * part_tiles + i
            parity_out[i] = parity_of(row)
            for c in cols:
                inverse[i, :, c] = 1.0 / inverse[i, :, c]
            return carry

        lax.fori_loop(0, part_tiles, body, 0, unroll=4)

    def halo(field):
        for c in cols:
            above = pltpu.roll(field[tiles, :, c], 1, 0)
            field[0, :, c] = jnp.where(row_in_tile == 0, 0.0, above)
            below = pltpu.roll(field[1, :, c], SUB - 1, 0)
            field[tiles + 1, :, c] = jnp.where(row_in_tile == SUB - 1, 0.0, below)

    def advance(field, before, j):
        here = [field[j + 1, :, c] for c in cols]
        west = [jnp.where(at_first, 0.0, pltpu.roll(here[-1], 1, 1))] + here[:-1]
        east = here[1:] + [jnp.where(at_last, 0.0, pltpu.roll(here[0], LANE - 1, 1))]
        moved = []
        for i, c in enumerate(cols):
            near = (field[j, :, c] + field[j + 2, :, c]) + (west[i] + east[i])
            value = centre[j, :, c] * here[i] + coef[j, :, c] * near
            if before is not None:
                value = value - before(j, c)
            moved.append(value)
        return moved

    def inner(field):
        return lambda j, c: field[j + 1, :, c]

    def sweep(body):
        def run(j, carry):
            body(j)
            return carry

        lax.fori_loop(0, tiles, run, 0, unroll=UNROLL)

    pair = range(num_probes)

    def start_fields(m):
        def body(j):
            for c in cols:
                value = lev[m, 1, j + 1, :, c]
                for p in pair:
                    d1[p, j + 1, :, c] = vec[p, j, :, c] * value

        sweep(body)
        halo(lev.at[m, 1])
        for p in pair:
            halo(d1.at[p])

    def levels_step(m, t):
        field = (lev.at[m, 1], u1, u2)[t]
        before = (inner(lev.at[m, 0]), inner(lev.at[m, 1]), inner(u1))[t]
        result = (u1, u2, u3)[t]

        def body(j):
            for c, value in zip(cols, advance(field, before, j)):
                result[j + 1, :, c] = value

        sweep(body)
        for c in cols:
            row = jnp.broadcast_to(source[m, t : t + 1, c], (SUB, LANE))
            result[1, :, c] = result[1, :, c] + jnp.where(row_in_tile == SUB // 2, row, 0.0)
        if t < 2:
            halo(result)

    def chosen(j, values, i):
        return jnp.where(parity_in[j] == 1, values[0][i], values[1][i])

    def forward(m, t):
        level = (u1, u2, u3)[t]
        delta = (d1, d2, d3)[t]
        delta_before = (None, d1, d2)[t]
        delta_next = (d2, d3, e4)[t]

        def body(j):
            values = []
            for p in pair:
                prior = None if delta_before is None else inner(delta_before.at[p])
                step = advance(delta.at[p], prior, j)
                for i, c in enumerate(cols):
                    step[i] = step[i] + vec[p, j, :, c] * level[j + 1, :, c]
                    if t == 2:
                        step[i] = weight[j, :, c] * step[i]
                    delta_next[p, j + 1, :, c] = step[i]
                values.append(step)
            if t == 2:
                for i, c in enumerate(cols):
                    gain = level[j + 1, :, c] * chosen(j, values, i)
                    if m:
                        gain = total[j, :, c] + gain
                    total[j, :, c] = gain

        sweep(body)
        for p in pair:
            halo(delta_next.at[p])

    def adjoint(m, t):
        field = (e4, e3, e2)[t]
        before = (None, e4, e3)[t]
        result = (e3, e2, None)[t]
        delta = (d3, d2, d1)[t]
        level = (u2, u1, lev.at[m, 1])[t]

        def body(j):
            values = []
            for p in pair:
                prior = None if before is None else inner(before.at[p])
                step = advance(field.at[p], prior, j)
                for i, c in enumerate(cols):
                    step[i] = step[i] + weight[j, :, c] * delta[p, j + 1, :, c]
                    if result is not None:
                        result[p, j + 1, :, c] = step[i]
                values.append(step)
            for i, c in enumerate(cols):
                total[j, :, c] = total[j, :, c] + level[j + 1, :, c] * chosen(j, values, i)

        sweep(body)
        if result is not None:
            for p in pair:
                halo(result.at[p])

    def piece(k, device):
        first = pl.multiple_of(device * share, share)
        return total.at[pl.ds(k * part_tiles, part_tiles), pl.ds(first, share), :]

    def start_swap():
        for k in range(num_shot_devices):
            for away in range(1, num_shot_devices):
                other = (shot + away) % num_shot_devices
                pltpu.make_async_remote_copy(
                    src_ref=piece(k, other),
                    dst_ref=partial.at[away - 1, :, pl.ds(k * share, share), :],
                    send_sem=swap_send.at[0],
                    recv_sem=swap_recv.at[away - 1],
                    device_id={"shot": other},
                    device_id_type=MESH,
                ).start()
            pltpu.make_async_copy(
                piece(k, shot), packed.at[:, pl.ds(k * share, share), :], pack_sem.at[0]
            ).start()

    def combine(j):
        at = pl.ds(j, block)
        value = packed[at]
        for away in range(1, num_shot_devices):
            value = value + partial[away - 1, at]
        value = tiled(shuffle(flat(value), collect_table)) * inverse[at]
        for p in pair:
            for i in range(block):
                keep = parity_out[j + i] != p % 2
                for n, c in enumerate(cols):
                    piece_of = value[i, :, n * LANE : (n + 1) * LANE] - coarse_in[p, j + i, :, c]
                    result_out[p, j + i, :, c] = jnp.where(keep, piece_of, 0.0)

    def deliver(p):
        for k in range(num_shot_devices):
            for e in range(share):
                pltpu.make_async_copy(
                    result_out.at[p, :, k * share + e, :],
                    out_hbm.at[p, pl.ds(e * tiles + k * part_tiles, part_tiles), :],
                    out_sem.at[0],
                ).start()

    work = []

    def add_work(run, ref=None, sem=None):
        def first():
            if ref is not None:
                await_bytes(ref, sem)
            run(0)

        work.append(first)
        for b in range(1, tiles // block):
            work.append(lambda b=b: run(b * block))

    work.append(prepare_sources)
    add_work(prepare_coefficient, coefficient_in, load_sem.at[0])
    add_work(prepare_weight, receiver_in, load_sem.at[1])
    add_work(prepare_vectors, probes_in, load_sem.at[2])

    def out_work():
        await_bytes(inverse, load_sem.at[3])
        prepare_out()
        await_bytes(coarse_in, load_sem.at[4])

    work.append(out_work)
    def gather_plan():
        plan = []
        for k in range(1, line):
            for m in range(members):
                plan.append(lambda k=k, m=m: column(m, k))
                if k == 1 and m + 1 < members:
                    plan.append(lambda m=m: own_ring(m + 1))
        ends = []
        for m in range(members):
            last = [lambda k=k, m=m: relay(m, k) for k in range(line)]
            if m in BY_LINE:
                last = [f for k in range(line) for f in (last[k], lambda k=k, m=m: across(m, k))]
            ends.append(last)
        return plan + ends[0], ends[1:]

    before, during = gather_plan()
    per = -(-len(work) // len(before))
    for step in before:
        step()
        for _ in range(per):
            if work:
                work.pop(0)()
    for rest in work:
        rest()
    for m in range(members):
        gather_end(m)
        plan = during[m] if m < len(during) else []
        stages = [lambda: start_fields(m)]
        stages += [lambda t=t: levels_step(m, t) for t in range(3)]
        stages += [lambda t=t: forward(m, t) for t in range(3)]
        stages += [lambda t=t: adjoint(m, t) for t in range(3)]
        for stage in stages:
            stage()
            if plan:
                plan.pop(0)()
        for step in plan:
            step()
    start_swap()
    await_bytes(packed, pack_sem.at[0])
    for away in range(1, num_shot_devices):
        await_bytes(partial.at[away - 1], swap_recv.at[away - 1])
    by_block(0, part_tiles // block, combine)
    for p in pair:
        deliver(p)
    await_bytes(partial, swap_send.at[0])
    sends_end()
    await_bytes(result_out, out_sem.at[0])


def on_device(
    num_shot_devices,
    num_probe_devices,
    probes,
    coarse_sample,
    coefficient,
    receiver,
    checkpoints,
    encodings,
    wavelet,
    bounds,
):
    members, levels, chunk, width = checkpoints.shape
    num_probes, num_rows, _ = probes.shape
    out_rows = coarse_sample.shape[1]
    tiles = num_rows // SUB
    line = num_probe_devices // INNER
    f32 = jnp.float32

    part_tiles = tiles // num_shot_devices
    whole_pieces = sum(2 * line + (1 if m in BY_LINE else line) for m in range(members))

    def plain(*lead):
        return pltpu.VMEM((*lead, tiles, SUB, width), f32)

    def ringed(*lead):
        return pltpu.VMEM((*lead, tiles + 2, SUB, width), f32)

    def part(*lead):
        return pltpu.VMEM((*lead, part_tiles, SUB, width), f32)

    others = num_shot_devices - 1
    anywhere = pl.BlockSpec(memory_space=pl.ANY)
    vmem = pl.BlockSpec(memory_space=pltpu.VMEM)
    return pl.pallas_call(
        functools.partial(kernel, num_shot_devices, num_probe_devices),
        out_shape=jax.ShapeDtypeStruct(coarse_sample.shape, f32),
        in_specs=[pl.BlockSpec(memory_space=pltpu.SMEM), vmem, vmem] + [anywhere] * 5,
        out_specs=anywhere,
        scratch_shapes=[
            pltpu.VMEM(checkpoints.shape, f32),
            pltpu.VMEM(checkpoints.shape, f32),
            plain(num_probes),
            part(num_probes),
            plain(),
            plain(),
            part(),
            pltpu.VMEM((width, width), jnp.bfloat16),
            pltpu.VMEM((width, width), jnp.bfloat16),
            pltpu.VMEM((tiles, SUB, LANE), jnp.int32),
            pltpu.VMEM((part_tiles, SUB, LANE), jnp.int32),
            plain(),
            plain(),
            plain(),
            plain(num_probes + 1),
            ringed(members, levels),
            pltpu.VMEM((whole_pieces, levels, chunk, width), f32),
            ringed(),
            ringed(),
            ringed(),
            ringed(num_probes),
            ringed(num_probes),
            ringed(num_probes),
            ringed(num_probes),
            ringed(num_probes),
            ringed(num_probes),
            plain(),
            part(),
            part(others),
            part(num_probes),
            pltpu.VMEM((members, SUB, width), f32),
            pltpu.SemaphoreType.DMA((5,)),
            pltpu.SemaphoreType.DMA((1 + members,)),
            pltpu.SemaphoreType.DMA((members, 4, line)),
            pltpu.SemaphoreType.DMA((members,)),
            pltpu.SemaphoreType.DMA((2,)),
            pltpu.SemaphoreType.DMA((1,)),
            pltpu.SemaphoreType.DMA((1,)),
            pltpu.SemaphoreType.DMA((1,)),
            pltpu.SemaphoreType.DMA((others,)),
        ],
        compiler_params=pltpu.CompilerParams(
            collective_id=0, has_side_effects=True, vmem_limit_bytes=60 * 1024 * 1024
        ),
    )(
        bounds,
        encodings,
        wavelet,
        probes,
        coarse_sample,
        coefficient,
        receiver,
        checkpoints,
    )


def solution(mesh):
    return jax.shard_map(
        functools.partial(on_device, mesh.shape["shot"], mesh.shape["probe"]),
        mesh=mesh,
        in_specs=(
            P("probe", None, None),
            P("probe", "shot", None),
            P(),
            P(),
            P("shot", None, "probe", None),
            P("shot", None),
            P(),
            P(),
        ),
        out_specs=P("probe", "shot", None),
        check_vma=False,
    )
```

```python
import functools

import jax
import jax.numpy as jnp
from jax import lax
from jax.experimental import pallas as pl
from jax.experimental.pallas import tpu as pltpu
from jax.sharding import PartitionSpec as P

MESH = pl.DeviceIdType.MESH
SUB = 8
LANE = 128
INNER = 4
UNROLL = 32


def kernel(
    num_shot_devices,
    num_probe_devices,
    bounds_ref,
    encodings_ref,
    wavelet_ref,
    probes_hbm,
    coarse_hbm,
    coefficient_hbm,
    receiver_hbm,
    checkpoints_hbm,
    out_hbm,
    own_in,
    own,
    probes_in,
    coarse_in,
    coefficient_in,
    receiver_in,
    inverse,
    spread_table,
    collect_table,
    parity_in,
    parity_out,
    coef,
    centre,
    weight,
    vec,
    lev,
    counter,
    u1,
    u2,
    u3,
    d1,
    d2,
    d3,
    e4,
    e3,
    e2,
    total,
    packed,
    partial,
    result_out,
    source,
    load_sem,
    own_sem,
    hop_sem,
    far_sem,
    send_sem,
    pack_sem,
    out_sem,
    swap_send,
    swap_recv,
):
    members, levels, chunk, width = checkpoints_hbm.shape
    num_probes, num_rows, _ = probes_hbm.shape
    out_rows = coarse_hbm.shape[1]
    tiles = num_rows // SUB
    groups = width // LANE
    cols = [pl.ds(c * LANE, LANE) for c in range(groups)]
    steps = wavelet_ref.shape[0]
    line = num_probe_devices // INNER
    share = SUB // num_shot_devices
    part_tiles = tiles // num_shot_devices
    by_line = (members - 1,)
    block = min(8, part_tiles)
    rows_of_block = block * SUB

    shot = lax.axis_index("shot")
    mine = lax.axis_index("probe")
    z = mine // INNER
    a = mine % INNER
    high, low = a // 2, a % 2
    right = 2 * low + (1 - high)
    left = 2 * (1 - low) + high

    places = {"a": a, "right": right, "left": left, "far": 3 - a}
    ids = {
        (dz, name): (z + dz) * INNER + place
        for dz in range(1 - line, line)
        for name, place in places.items()
    }
    exists = {dz: (z + dz >= 0) & (z + dz < line) for dz in range(1 - line, line)}
    def slot(m, src, t=None):
        first = src * chunk
        rows = pl.ds(first % tiles + 1, chunk)
        if t is None:
            return lev.at[m, :, rows, first // tiles, :]
        return lev.at[m, t, rows, first // tiles, :]

    load_own = pltpu.make_async_copy(checkpoints_hbm, own_in, own_sem.at[0])
    load_own.start()

    barrier = pltpu.get_barrier_semaphore()

    def greet(device):
        pl.semaphore_signal(barrier, inc=1, device_id=device, device_id_type=MESH)

    greet({"probe": ids[0, "right"]})
    greet({"probe": ids[0, "left"]})

    for dz in range(1 - line, line):
        if dz:

            @pl.when(exists[dz])
            def _(dz=dz):
                greet({"probe": ids[dz, "a"]})

    for away in range(1, num_shot_devices):
        greet({"shot": (shot + away) % num_shot_devices})

    def build_table(table, spread):
        def body(b, carry):
            rows = pl.ds(pl.multiple_of(b * LANE, LANE), LANE)
            row = lax.broadcasted_iota(jnp.int32, (LANE, width), 0) + b * LANE
            col = lax.broadcasted_iota(jnp.int32, (LANE, width), 1)
            fine, place = (row, col) if spread else (col, row)
            match = fine == groups * (place % LANE) + place // LANE
            table[rows, :] = jnp.where(match, 1.0, 0.0).astype(jnp.bfloat16)
            return carry

        lax.fori_loop(0, groups, body, 0)

    def shuffle(x, table):
        high = x.astype(jnp.bfloat16)
        rest = x - high.astype(jnp.float32)
        middle = rest.astype(jnp.bfloat16)
        low = (rest - middle.astype(jnp.float32)).astype(jnp.bfloat16)
        moved = [
            jnp.dot(piece, table[...], preferred_element_type=jnp.float32)
            for piece in (high, middle, low)
        ]
        return moved[0] + (moved[1] + moved[2])

    build_table(spread_table, True)
    load_own.wait()
    count = members * levels * chunk
    own[...] = shuffle(own_in[...].reshape(count, width), spread_table).reshape(own.shape)
    pl.semaphore_wait(barrier, line - 1 + 2 + num_shot_devices - 1)

    def send(source, target, place, sem, which=0):
        pltpu.make_async_remote_copy(
            src_ref=source,
            dst_ref=place,
            send_sem=send_sem.at[which],
            recv_sem=sem,
            device_id={"probe": ids[target]},
            device_id_type=MESH,
        ).start()

    def await_bytes(ref, sem):
        pltpu.make_async_copy(ref, ref, sem).wait()

    def guarded(cond, fun):
        if cond is None:
            fun()
        else:
            pl.when(cond)(fun)

    def sides(k):
        if k == 0:
            return ((0, None),)
        return ((-k, exists[-k]), (k, exists[k]))

    def own_to_place(m):
        return pltpu.make_async_copy(own.at[m], slot(m, mine), own_sem.at[1 + m])

    def along_line(m, kind, name, source, dz, ways):
        place = slot(m, ids[dz, name])
        for way in ways:
            pl.when(exists[way])(
                lambda way=way: send(source, (way, "a"), place, hop_sem.at[m, kind, z + dz], 1)
            )

    def to_ring(m, dz):
        source = own.at[m] if dz == 0 else slot(m, ids[dz, "a"])
        place = slot(m, ids[dz, "a"])
        send(source, (0, "right"), place, hop_sem.at[m, 1, z + dz])
        send(source, (0, "left"), place, hop_sem.at[m, 2, z + dz])

    def own_line(m):
        along_line(m, 0, "a", own.at[m], 0, (1, -1))

    def own_ring(m):
        to_ring(m, 0)

    def passing(m, kind, name, k, after):
        for dz, cond in sides(k):

            def run(dz=dz):
                place = slot(m, ids[dz, name])
                await_bytes(place, hop_sem.at[m, kind, z + dz])
                if k == 0:
                    along_line(m, kind, name, place, 0, (1, -1))
                elif k < line - 1:
                    along_line(m, kind, name, place, dz, (1,) if dz < 0 else (-1,))
                after(dz)

            guarded(cond, run)

    def column(m, k):
        passing(m, 0, "a", k, lambda dz: to_ring(m, dz))

    def across(m, k):
        passing(m, 3, "far", k, lambda dz: None)

    def relay(m, k):
        for dz, cond in sides(k):

            def run(dz=dz):
                last = hop_sem.at[m, 3, z] if m in by_line else far_sem.at[m]
                await_bytes(slot(m, ids[dz, "left"]), hop_sem.at[m, 1, z + dz])
                if k == 0 or m not in by_line:
                    place = slot(m, ids[dz, "left"], 0)
                    send(place, (0, "right"), place, last)
                await_bytes(slot(m, ids[dz, "right"]), hop_sem.at[m, 2, z + dz])
                if k == 0 or m not in by_line:
                    place = slot(m, ids[dz, "right"], 1)
                    send(place, (0, "left"), place, last)

            guarded(cond, run)

    def gather_end(m):
        if m not in by_line:
            await_bytes(counter.at[pl.ds(0, line)], far_sem.at[m])
        own_to_place(m).wait()

    def line_sends_end():
        for m in range(members):
            for dz in (1, -1):
                for _ in range(2 if m in by_line else 1):
                    for k in range(line - 1):
                        cond = exists[dz] if k == 0 else exists[dz] & exists[-k * dz]
                        pl.when(cond)(lambda: await_bytes(own.at[0], send_sem.at[1]))

    own_line(0)
    for m in range(members):
        own_ring(m)
    for m in range(1, members):
        own_line(m)
    for m in range(members):
        own_to_place(m).start()

    def strided_load(src, dst, sem):
        for k in range(SUB):
            pltpu.make_async_copy(src.at[pl.ds(k * tiles, tiles), :], dst.at[:, k, :], sem).start()

    strided_load(coefficient_hbm, coefficient_in, load_sem.at[0])
    strided_load(receiver_hbm, receiver_in, load_sem.at[1])
    for p in range(num_probes):
        strided_load(probes_hbm.at[p], probes_in.at[p], load_sem.at[2])
    build_table(collect_table, False)
    for k in range(num_shot_devices):
        for e in range(share):
            first = pl.multiple_of(e * tiles + k * part_tiles, SUB)
            near = pl.multiple_of(shot * out_rows + e * tiles + k * part_tiles, SUB)
            pltpu.make_async_copy(
                coefficient_hbm.at[pl.ds(near, part_tiles), :],
                inverse.at[:, k * share + e, :],
                load_sem.at[3],
            ).start()
            for p in range(num_probes):
                pltpu.make_async_copy(
                    coarse_hbm.at[p, pl.ds(first, part_tiles), :],
                    coarse_in.at[p, :, k * share + e, :],
                    load_sem.at[4],
                ).start()

    row_in_tile = lax.broadcasted_iota(jnp.int32, (SUB, LANE), 0)
    lane_index = lax.broadcasted_iota(jnp.int32, (SUB, LANE), 1)
    at_first = lane_index == 0
    at_last = lane_index == LANE - 1

    def parity_of(rows):
        count = jnp.zeros((SUB, LANE), jnp.int32)
        for b in range(1, bounds_ref.shape[0] - 1):
            count = count + jnp.where(rows >= bounds_ref[b], 1, 0)
        return count % 2

    def prepare_sources():
        shots = wavelet_ref.shape[1]
        spacing = width // shots
        k = lax.broadcasted_iota(jnp.int32, (shots, width), 0)
        position = k * width // shots + spacing // 2
        index = lax.broadcasted_iota(jnp.int32, (shots, width), 1)
        onehot = jnp.where(position == groups * (index % LANE) + index // LANE, 1.0, 0.0)
        for m in range(members):
            amplitude = encodings_ref[m : m + 1, :].astype(jnp.float32) * wavelet_ref[...]
            source[m, 0:steps, :] = jnp.dot(
                amplitude,
                onehot,
                precision=lax.Precision.HIGHEST,
                preferred_element_type=jnp.float32,
            )

    def flat(x):
        return x.reshape(rows_of_block, width)

    def tiled(x):
        return x.reshape(block, SUB, width)

    def prepare_coefficient(j):
        at = pl.ds(j, block)
        value = tiled(shuffle(flat(coefficient_in[at]), spread_table))
        coef[at] = value
        centre[at] = 2.0 - 4.0 * value

    def prepare_weight(j):
        at = pl.ds(j, block)
        seen = tiled(shuffle(flat(receiver_in[at]), spread_table))
        weight[at] = coef[at] * (seen * seen)

    def prepare_vectors(j):
        at = pl.ds(j, block)
        rows = []
        for i in range(block):
            parity = parity_of(row_in_tile * tiles + (j + i))
            parity_in[j + i] = parity
            rows.append(
                jnp.concatenate(
                    [
                        jnp.where(parity == 0, probes_in[0, j + i, :, c], probes_in[1, j + i, :, c])
                        for c in cols
                    ],
                    axis=1,
                )
            )
        both = tiled(shuffle(jnp.concatenate(rows, axis=0), spread_table))
        vec[2, at] = both
        for i in range(block):
            even = parity_in[j + i] == 0
            for c in cols:
                value = vec[2, j + i, :, c]
                vec[0, j + i, :, c] = jnp.where(even, value, 0.0)
                vec[1, j + i, :, c] = jnp.where(even, 0.0, value)

    def prepare_out():
        def body(i, carry):
            row = shot * out_rows + (row_in_tile % share) * tiles + (row_in_tile // share) * part_tiles + i
            parity_out[i] = parity_of(row)
            for c in cols:
                inverse[i, :, c] = 1.0 / inverse[i, :, c]
            return carry

        lax.fori_loop(0, part_tiles, body, 0, unroll=4)

    def halo(field):
        for c in cols:
            above = pltpu.roll(field[tiles, :, c], 1, 0)
            field[0, :, c] = jnp.where(row_in_tile == 0, 0.0, above)
            below = pltpu.roll(field[1, :, c], SUB - 1, 0)
            field[tiles + 1, :, c] = jnp.where(row_in_tile == SUB - 1, 0.0, below)

    def advance(field, before, j):
        here = [field[j + 1, :, c] for c in cols]
        west = [jnp.where(at_first, 0.0, pltpu.roll(here[-1], 1, 1))] + here[:-1]
        east = here[1:] + [jnp.where(at_last, 0.0, pltpu.roll(here[0], LANE - 1, 1))]
        moved = []
        for i, c in enumerate(cols):
            near = (field[j, :, c] + field[j + 2, :, c]) + (west[i] + east[i])
            value = centre[j, :, c] * here[i] + coef[j, :, c] * near
            if before is not None:
                value = value - before(j, c)
            moved.append(value)
        return moved

    def inner(field):
        return lambda j, c: field[j + 1, :, c]

    def sweep(body, first=0, last=tiles):
        def run(j, carry):
            body(j)
            return carry

        lax.fori_loop(first, last, run, 0, unroll=min(UNROLL, last - first))

    pair = range(num_probes)

    def start_fields(m):
        def body(j):
            for c in cols:
                value = lev[m, 1, j + 1, :, c]
                for p in pair:
                    d1[p, j + 1, :, c] = vec[p, j, :, c] * value

        sweep(body)
        halo(lev.at[m, 1])
        for p in pair:
            halo(d1.at[p])

    def levels_step(m, t):
        field = (lev.at[m, 1], u1, u2)[t]
        before = (inner(lev.at[m, 0]), inner(lev.at[m, 1]), inner(u1))[t]
        result = (u1, u2, u3)[t]

        def body(j):
            for c, value in zip(cols, advance(field, before, j)):
                result[j + 1, :, c] = value

        sweep(body)
        for c in cols:
            row = jnp.broadcast_to(source[m, t : t + 1, c], (SUB, LANE))
            result[1, :, c] = result[1, :, c] + jnp.where(row_in_tile == SUB // 2, row, 0.0)
        if t < 2:
            halo(result)

    def chosen(j, values, i):
        return jnp.where(parity_in[j] == 1, values[0][i], values[1][i])

    def forward(m, t):
        level = (u1, u2, u3)[t]
        delta = (d1, d2, d3)[t]
        delta_before = (None, d1, d2)[t]
        delta_next = (d2, d3, e4)[t]

        def body(j):
            values = []
            for p in pair:
                prior = None if delta_before is None else inner(delta_before.at[p])
                step = advance(delta.at[p], prior, j)
                for i, c in enumerate(cols):
                    step[i] = step[i] + vec[p, j, :, c] * level[j + 1, :, c]
                    if t == 2:
                        step[i] = weight[j, :, c] * step[i]
                    delta_next[p, j + 1, :, c] = step[i]
                values.append(step)
            if t == 2:
                for i, c in enumerate(cols):
                    total[j, :, c] = total[j, :, c] + level[j + 1, :, c] * chosen(j, values, i)

        sweep(body)
        for p in pair:
            halo(delta_next.at[p])

    def adjoint(m, t):
        field = (e4, e3, e2)[t]
        before = (None, e4, e3)[t]
        result = (e3, e2, None)[t]
        delta = (d3, d2, d1)[t]
        level = (u2, u1, lev.at[m, 1])[t]

        def body(j):
            values = []
            for p in pair:
                prior = None if before is None else inner(before.at[p])
                step = advance(field.at[p], prior, j)
                for i, c in enumerate(cols):
                    step[i] = step[i] + weight[j, :, c] * delta[p, j + 1, :, c]
                    if result is not None:
                        result[p, j + 1, :, c] = step[i]
                values.append(step)
            for i, c in enumerate(cols):
                total[j, :, c] = total[j, :, c] + level[j + 1, :, c] * chosen(j, values, i)

        if result is None:
            for k in range(num_shot_devices):
                sweep(body, k * part_tiles, (k + 1) * part_tiles)
                pl.when(m == members - 1)(lambda k=k: start_swap(k))
        else:
            sweep(body)
        if result is not None:
            for p in pair:
                halo(result.at[p])

    def piece(k, device):
        first = pl.multiple_of(device * share, share)
        return total.at[pl.ds(k * part_tiles, part_tiles), pl.ds(first, share), :]

    def start_swap(k):
        for away in range(1, num_shot_devices):
            other = (shot + away) % num_shot_devices
            pltpu.make_async_remote_copy(
                src_ref=piece(k, other),
                dst_ref=partial.at[away - 1, :, pl.ds(k * share, share), :],
                send_sem=swap_send.at[0],
                recv_sem=swap_recv.at[away - 1],
                device_id={"shot": other},
                device_id_type=MESH,
            ).start()
        pltpu.make_async_copy(
            piece(k, shot), packed.at[:, pl.ds(k * share, share), :], pack_sem.at[0]
        ).start()

    def combine(j):
        at = pl.ds(j, block)
        value = packed[at]
        for away in range(1, num_shot_devices):
            value = value + partial[away - 1, at]
        value = tiled(shuffle(flat(value), collect_table)) * inverse[at]
        for p in pair:
            for i in range(block):
                keep = parity_out[j + i] != p % 2
                for n, c in enumerate(cols):
                    piece_of = value[i, :, n * LANE : (n + 1) * LANE] - coarse_in[p, j + i, :, c]
                    result_out[p, j + i, :, c] = jnp.where(keep, piece_of, 0.0)

    def deliver(j):
        for p in pair:
            for k in range(num_shot_devices):
                for e in range(share):
                    first = e * tiles + k * part_tiles + j
                    pltpu.make_async_copy(
                        result_out.at[p, pl.ds(j, block), k * share + e, :],
                        out_hbm.at[p, pl.ds(first, block), :],
                        out_sem.at[0],
                    ).start()

    work = []

    def add_work(run, ref=None, sem=None):
        def first():
            if ref is not None:
                await_bytes(ref, sem)
            run(0)

        work.append(first)
        for b in range(1, tiles // block):
            work.append(lambda b=b: run(b * block))

    def clear_total():
        total[...] = jnp.zeros_like(total)

    work.append(clear_total)
    work.append(prepare_sources)
    add_work(prepare_coefficient, coefficient_in, load_sem.at[0])
    add_work(prepare_weight, receiver_in, load_sem.at[1])
    add_work(prepare_vectors, probes_in, load_sem.at[2])

    def out_work():
        await_bytes(inverse, load_sem.at[3])
        prepare_out()
        await_bytes(coarse_in, load_sem.at[4])

    work.insert(1, out_work)
    def gather_plan():
        last = members - 1
        plan = [lambda: column(0, 1), lambda: relay(last, 0)]
        plan += [lambda: column(last, 1), lambda: relay(0, 0)]
        for k in range(2, line):
            plan += [lambda k=k: column(0, k), lambda k=k: across(last, k - 2)]
            plan += [lambda k=k: column(last, k), lambda k=k: relay(0, k - 1)]
        plan.append(lambda: relay(0, line - 1))
        rest = [lambda: across(last, line - 1)]
        rest += [lambda k=k: relay(last, k) for k in range(1, line)]
        return plan, rest

    before, after = gather_plan()
    while len(work) > len(before):
        work.pop(0)()
    for step in before:
        step()
        if work:
            work.pop(0)()
    for rest in work:
        rest()
    def arrived(m):
        if m == members - 1:
            for step in after:
                step()
            line_sends_end()
        gather_end(m)
        if m == 0:
            across(members - 1, line - 2)

    def member(m, carry):
        for i in range(members):
            pl.when(m == i)(lambda i=i: arrived(i))
        start_fields(m)
        for t in range(3):
            levels_step(m, t)
        for t in range(3):
            forward(m, t)
        for t in range(3):
            adjoint(m, t)
        return carry

    lax.fori_loop(0, members, member, 0)
    await_bytes(packed, pack_sem.at[0])
    for away in range(1, num_shot_devices):
        await_bytes(partial.at[away - 1], swap_recv.at[away - 1])
    for b in range(part_tiles // block):
        combine(b * block)
        deliver(b * block)
    await_bytes(partial, swap_send.at[0])
    await_bytes(counter, send_sem.at[0])
    await_bytes(result_out, out_sem.at[0])


def on_device(
    num_shot_devices,
    num_probe_devices,
    probes,
    coarse_sample,
    coefficient,
    receiver,
    checkpoints,
    encodings,
    wavelet,
    bounds,
):
    members, levels, chunk, width = checkpoints.shape
    num_probes, num_rows, _ = probes.shape
    out_rows = coarse_sample.shape[1]
    tiles = num_rows // SUB
    line = num_probe_devices // INNER
    f32 = jnp.float32

    part_tiles = tiles // num_shot_devices
    whole_pieces = members * 3 * line - (line - 1)

    def plain(*lead):
        return pltpu.VMEM((*lead, tiles, SUB, width), f32)

    def ringed(*lead):
        return pltpu.VMEM((*lead, tiles + 2, SUB, width), f32)

    def part(*lead):
        return pltpu.VMEM((*lead, part_tiles, SUB, width), f32)

    others = num_shot_devices - 1
    anywhere = pl.BlockSpec(memory_space=pl.ANY)
    vmem = pl.BlockSpec(memory_space=pltpu.VMEM)
    return pl.pallas_call(
        functools.partial(kernel, num_shot_devices, num_probe_devices),
        out_shape=jax.ShapeDtypeStruct(coarse_sample.shape, f32),
        in_specs=[pl.BlockSpec(memory_space=pltpu.SMEM), vmem, vmem] + [anywhere] * 5,
        out_specs=anywhere,
        scratch_shapes=[
            pltpu.VMEM(checkpoints.shape, f32),
            pltpu.VMEM(checkpoints.shape, f32),
            plain(num_probes),
            part(num_probes),
            plain(),
            plain(),
            part(),
            pltpu.VMEM((width, width), jnp.bfloat16),
            pltpu.VMEM((width, width), jnp.bfloat16),
            pltpu.VMEM((tiles, SUB, LANE), jnp.int32),
            pltpu.VMEM((part_tiles, SUB, LANE), jnp.int32),
            plain(),
            plain(),
            plain(),
            plain(num_probes + 1),
            ringed(members, levels),
            pltpu.VMEM((whole_pieces, levels, chunk, width), f32),
            ringed(),
            ringed(),
            ringed(),
            ringed(num_probes),
            ringed(num_probes),
            ringed(num_probes),
            ringed(num_probes),
            ringed(num_probes),
            ringed(num_probes),
            plain(),
            part(),
            part(others),
            part(num_probes),
            pltpu.VMEM((members, SUB, width), f32),
            pltpu.SemaphoreType.DMA((5,)),
            pltpu.SemaphoreType.DMA((1 + members,)),
            pltpu.SemaphoreType.DMA((members, 4, line)),
            pltpu.SemaphoreType.DMA((members,)),
            pltpu.SemaphoreType.DMA((2,)),
            pltpu.SemaphoreType.DMA((1,)),
            pltpu.SemaphoreType.DMA((1,)),
            pltpu.SemaphoreType.DMA((1,)),
            pltpu.SemaphoreType.DMA((others,)),
        ],
        compiler_params=pltpu.CompilerParams(
            collective_id=0, has_side_effects=True, vmem_limit_bytes=60 * 1024 * 1024
        ),
    )(
        bounds,
        encodings,
        wavelet,
        probes,
        coarse_sample,
        coefficient,
        receiver,
        checkpoints,
    )


def solution(mesh):
    return jax.shard_map(
        functools.partial(on_device, mesh.shape["shot"], mesh.shape["probe"]),
        mesh=mesh,
        in_specs=(
            P("probe", None, None),
            P("probe", "shot", None),
            P(),
            P(),
            P("shot", None, "probe", None),
            P("shot", None),
            P(),
            P(),
        ),
        out_specs=P("probe", "shot", None),
        check_vma=False,
    )
```

```python
import functools

import jax
import jax.numpy as jnp
from jax import lax
from jax.experimental import pallas as pl
from jax.experimental.pallas import tpu as pltpu
from jax.sharding import PartitionSpec as P

MESH = pl.DeviceIdType.MESH
SUB = 8
LANE = 128
INNER = 4
UNROLL = 32


def kernel(
    num_shot_devices,
    num_probe_devices,
    bounds_ref,
    encodings_ref,
    wavelet_ref,
    probes_hbm,
    coarse_hbm,
    coefficient_hbm,
    receiver_hbm,
    checkpoints_hbm,
    out_hbm,
    own_in,
    own,
    probes_in,
    coarse_in,
    coefficient_in,
    receiver_in,
    inverse,
    spread_table,
    collect_table,
    parity_in,
    parity_out,
    coef,
    centre,
    weight,
    vec,
    lev,
    counter,
    u1,
    u2,
    u3,
    d1,
    d2,
    d3,
    e4,
    e3,
    e2,
    total,
    packed,
    partial,
    result_out,
    source,
    load_sem,
    own_sem,
    hop_sem,
    far_sem,
    send_sem,
    pack_sem,
    out_sem,
    swap_send,
    swap_recv,
):
    members, levels, chunk, width = checkpoints_hbm.shape
    num_probes, num_rows, _ = probes_hbm.shape
    out_rows = coarse_hbm.shape[1]
    tiles = num_rows // SUB
    groups = width // LANE
    cols = [pl.ds(c * LANE, LANE) for c in range(groups)]
    steps = wavelet_ref.shape[0]
    line = num_probe_devices // INNER
    share = SUB // num_shot_devices
    part_tiles = tiles // num_shot_devices
    by_line = (members - 1,)
    block = min(8, part_tiles)
    rows_of_block = block * SUB

    shot = lax.axis_index("shot")
    mine = lax.axis_index("probe")
    z = mine // INNER
    a = mine % INNER
    high, low = a // 2, a % 2
    right = 2 * low + (1 - high)
    left = 2 * (1 - low) + high

    places = {"a": a, "right": right, "left": left, "far": 3 - a}
    ids = {
        (dz, name): (z + dz) * INNER + place
        for dz in range(1 - line, line)
        for name, place in places.items()
    }
    exists = {dz: (z + dz >= 0) & (z + dz < line) for dz in range(1 - line, line)}
    def slot(m, src, t=None):
        first = src * chunk
        rows = pl.ds(first % tiles + 1, chunk)
        if t is None:
            return lev.at[m, :, rows, first // tiles, :]
        return lev.at[m, t, rows, first // tiles, :]

    load_own = pltpu.make_async_copy(checkpoints_hbm, own_in, own_sem.at[0])
    load_own.start()

    barrier = pltpu.get_barrier_semaphore()

    def greet(device):
        pl.semaphore_signal(barrier, inc=1, device_id=device, device_id_type=MESH)

    greet({"probe": ids[0, "right"]})
    greet({"probe": ids[0, "left"]})

    for dz in range(1 - line, line):
        if dz:

            @pl.when(exists[dz])
            def _(dz=dz):
                greet({"probe": ids[dz, "a"]})

    for away in range(1, num_shot_devices):
        greet({"shot": (shot + away) % num_shot_devices})

    def build_table(table, spread):
        def body(b, carry):
            rows = pl.ds(pl.multiple_of(b * LANE, LANE), LANE)
            row = lax.broadcasted_iota(jnp.int32, (LANE, width), 0) + b * LANE
            col = lax.broadcasted_iota(jnp.int32, (LANE, width), 1)
            fine, place = (row, col) if spread else (col, row)
            match = fine == groups * (place % LANE) + place // LANE
            table[rows, :] = jnp.where(match, 1.0, 0.0).astype(jnp.bfloat16)
            return carry

        lax.fori_loop(0, groups, body, 0)

    def shuffle(x, table):
        high = x.astype(jnp.bfloat16)
        rest = x - high.astype(jnp.float32)
        middle = rest.astype(jnp.bfloat16)
        low = (rest - middle.astype(jnp.float32)).astype(jnp.bfloat16)
        moved = [
            jnp.dot(piece, table[...], preferred_element_type=jnp.float32)
            for piece in (high, middle, low)
        ]
        return moved[0] + (moved[1] + moved[2])

    build_table(spread_table, True)
    load_own.wait()
    count = members * levels * chunk
    own[...] = shuffle(own_in[...].reshape(count, width), spread_table).reshape(own.shape)
    pl.semaphore_wait(barrier, line - 1 + 2 + num_shot_devices - 1)

    def send(source, target, place, sem, which=0):
        pltpu.make_async_remote_copy(
            src_ref=source,
            dst_ref=place,
            send_sem=send_sem.at[which],
            recv_sem=sem,
            device_id={"probe": ids[target]},
            device_id_type=MESH,
        ).start()

    def await_bytes(ref, sem):
        pltpu.make_async_copy(ref, ref, sem).wait()

    def guarded(cond, fun):
        if cond is None:
            fun()
        else:
            pl.when(cond)(fun)

    def sides(k):
        if k == 0:
            return ((0, None),)
        return ((-k, exists[-k]), (k, exists[k]))

    def own_to_place(m):
        return pltpu.make_async_copy(own.at[m], slot(m, mine), own_sem.at[1 + m])

    def along_line(m, t, kind, name, source, dz, ways):
        place = slot(m, ids[dz, name], t)
        sem = hop_sem.at[m, kind, z + dz, t or 0]
        for way in ways:
            pl.when(exists[way])(
                lambda way=way: send(place if source is None else source, (way, "a"), place, sem, 1)
            )

    def relayed(m, dz):
        return dz == 0 or m not in by_line

    def to_ring(m, dz, t):
        source = own.at[m, t] if dz == 0 else slot(m, ids[dz, "a"], t)
        place = slot(m, ids[dz, "a"], t)
        for kind, name in ((1, "right"), (2, "left")):
            passed_on = relayed(m, dz) and t == kind - 1
            sem = hop_sem.at[m, kind, z + dz, 0] if passed_on else far_sem.at[m]
            send(source, (0, name), place, sem)

    def own_line(m):
        for t in range(levels):
            along_line(m, t, 0, "a", own.at[m, t], 0, (1, -1))

    def own_ring(m):
        for t in range(levels):
            to_ring(m, 0, t)

    def onward(k, dz):
        if k == 0:
            return (1, -1)
        if k < line - 1:
            return (1,) if dz < 0 else (-1,)
        return ()

    def column(m, k):
        for t in range(levels):
            for dz, cond in sides(k):

                def run(dz=dz, t=t):
                    await_bytes(slot(m, ids[dz, "a"], t), hop_sem.at[m, 0, z + dz, t])
                    along_line(m, t, 0, "a", None, dz, onward(k, dz))
                    to_ring(m, dz, t)

                guarded(cond, run)

    def across(m, k):
        for dz, cond in sides(k):

            def run(dz=dz):
                await_bytes(slot(m, ids[dz, "far"]), hop_sem.at[m, 3, z + dz, 0])
                along_line(m, None, 3, "far", None, dz, onward(k, dz))

            guarded(cond, run)

    def relay(m, k):
        for dz, cond in sides(k):

            def run(dz=dz):
                last = hop_sem.at[m, 3, z, 0] if m in by_line else far_sem.at[m]
                for t, (name, way) in enumerate((("left", "right"), ("right", "left"))):
                    place = slot(m, ids[dz, name], t)
                    await_bytes(place, hop_sem.at[m, 1 + t, z + dz, 0])
                    send(place, (0, way), place, last)

            guarded(cond, run)

    def gather_end(m):
        pieces = 2 * line - 1 if m in by_line else 2 * line
        await_bytes(counter.at[pl.ds(0, pieces)], far_sem.at[m])
        own_to_place(m).wait()

    def line_sends_end():
        for m in range(members):
            for dz in (1, -1):
                for _ in range(2 if m in by_line else 1):
                    for k in range(line - 1):
                        cond = exists[dz] if k == 0 else exists[dz] & exists[-k * dz]
                        pl.when(cond)(lambda: await_bytes(own.at[0], send_sem.at[1]))

    own_ring(0)
    for m in range(members):
        own_line(m)
    for m in range(1, members):
        own_ring(m)
    for m in range(members):
        own_to_place(m).start()

    def strided_load(src, dst, sem):
        for k in range(SUB):
            pltpu.make_async_copy(src.at[pl.ds(k * tiles, tiles), :], dst.at[:, k, :], sem).start()

    strided_load(coefficient_hbm, coefficient_in, load_sem.at[0])
    strided_load(receiver_hbm, receiver_in, load_sem.at[1])
    for p in range(num_probes):
        strided_load(probes_hbm.at[p], probes_in.at[p], load_sem.at[2])
    build_table(collect_table, False)
    for k in range(num_shot_devices):
        for e in range(share):
            first = pl.multiple_of(e * tiles + k * part_tiles, SUB)
            near = pl.multiple_of(shot * out_rows + e * tiles + k * part_tiles, SUB)
            pltpu.make_async_copy(
                coefficient_hbm.at[pl.ds(near, part_tiles), :],
                inverse.at[:, k * share + e, :],
                load_sem.at[3],
            ).start()
            for p in range(num_probes):
                pltpu.make_async_copy(
                    coarse_hbm.at[p, pl.ds(first, part_tiles), :],
                    coarse_in.at[p, :, k * share + e, :],
                    load_sem.at[4],
                ).start()

    row_in_tile = lax.broadcasted_iota(jnp.int32, (SUB, LANE), 0)
    lane_index = lax.broadcasted_iota(jnp.int32, (SUB, LANE), 1)
    at_first = lane_index == 0
    at_last = lane_index == LANE - 1

    def parity_of(rows):
        count = jnp.zeros((SUB, LANE), jnp.int32)
        for b in range(1, bounds_ref.shape[0] - 1):
            count = count + jnp.where(rows >= bounds_ref[b], 1, 0)
        return count % 2

    def prepare_sources():
        shots = wavelet_ref.shape[1]
        spacing = width // shots
        k = lax.broadcasted_iota(jnp.int32, (shots, width), 0)
        position = k * width // shots + spacing // 2
        index = lax.broadcasted_iota(jnp.int32, (shots, width), 1)
        onehot = jnp.where(position == groups * (index % LANE) + index // LANE, 1.0, 0.0)
        for m in range(members):
            amplitude = encodings_ref[m : m + 1, :].astype(jnp.float32) * wavelet_ref[...]
            source[m, 0:steps, :] = jnp.dot(
                amplitude,
                onehot,
                precision=lax.Precision.HIGHEST,
                preferred_element_type=jnp.float32,
            )

    def flat(x):
        return x.reshape(rows_of_block, width)

    def tiled(x):
        return x.reshape(block, SUB, width)

    def prepare_coefficient(j):
        at = pl.ds(j, block)
        value = tiled(shuffle(flat(coefficient_in[at]), spread_table))
        coef[at] = value
        centre[at] = 2.0 - 4.0 * value

    def prepare_weight(j):
        at = pl.ds(j, block)
        seen = tiled(shuffle(flat(receiver_in[at]), spread_table))
        weight[at] = coef[at] * (seen * seen)

    def prepare_vectors(j):
        at = pl.ds(j, block)
        rows = []
        for i in range(block):
            parity = parity_of(row_in_tile * tiles + (j + i))
            parity_in[j + i] = parity
            rows.append(
                jnp.concatenate(
                    [
                        jnp.where(parity == 0, probes_in[0, j + i, :, c], probes_in[1, j + i, :, c])
                        for c in cols
                    ],
                    axis=1,
                )
            )
        both = tiled(shuffle(jnp.concatenate(rows, axis=0), spread_table))
        vec[2, at] = both
        for i in range(block):
            even = parity_in[j + i] == 0
            for c in cols:
                value = vec[2, j + i, :, c]
                vec[0, j + i, :, c] = jnp.where(even, value, 0.0)
                vec[1, j + i, :, c] = jnp.where(even, 0.0, value)

    def prepare_out():
        def body(i, carry):
            row = shot * out_rows + (row_in_tile % share) * tiles + (row_in_tile // share) * part_tiles + i
            parity_out[i] = parity_of(row)
            for c in cols:
                inverse[i, :, c] = 1.0 / inverse[i, :, c]
            return carry

        lax.fori_loop(0, part_tiles, body, 0, unroll=4)

    def halo(field):
        for c in cols:
            above = pltpu.roll(field[tiles, :, c], 1, 0)
            field[0, :, c] = jnp.where(row_in_tile == 0, 0.0, above)
            below = pltpu.roll(field[1, :, c], SUB - 1, 0)
            field[tiles + 1, :, c] = jnp.where(row_in_tile == SUB - 1, 0.0, below)

    def advance(field, before, j):
        here = [field[j + 1, :, c] for c in cols]
        west = [jnp.where(at_first, 0.0, pltpu.roll(here[-1], 1, 1))] + here[:-1]
        east = here[1:] + [jnp.where(at_last, 0.0, pltpu.roll(here[0], LANE - 1, 1))]
        moved = []
        for i, c in enumerate(cols):
            near = (field[j, :, c] + field[j + 2, :, c]) + (west[i] + east[i])
            value = centre[j, :, c] * here[i] + coef[j, :, c] * near
            if before is not None:
                value = value - before(j, c)
            moved.append(value)
        return moved

    def inner(field):
        return lambda j, c: field[j + 1, :, c]

    def sweep(body, first=0, last=tiles):
        def run(j, carry):
            body(j)
            return carry

        lax.fori_loop(first, last, run, 0, unroll=min(UNROLL, last - first))

    pair = range(num_probes)

    def start_fields(m):
        def body(j):
            for c in cols:
                value = lev[m, 1, j + 1, :, c]
                for p in pair:
                    d1[p, j + 1, :, c] = vec[p, j, :, c] * value

        sweep(body)
        halo(lev.at[m, 1])
        for p in pair:
            halo(d1.at[p])

    def levels_step(m, t):
        field = (lev.at[m, 1], u1, u2)[t]
        before = (inner(lev.at[m, 0]), inner(lev.at[m, 1]), inner(u1))[t]
        result = (u1, u2, u3)[t]

        def body(j):
            for c, value in zip(cols, advance(field, before, j)):
                result[j + 1, :, c] = value

        sweep(body)
        for c in cols:
            row = jnp.broadcast_to(source[m, t : t + 1, c], (SUB, LANE))
            result[1, :, c] = result[1, :, c] + jnp.where(row_in_tile == SUB // 2, row, 0.0)
        if t < 2:
            halo(result)

    def chosen(j, values, i):
        return jnp.where(parity_in[j] == 1, values[0][i], values[1][i])

    def forward(m, t):
        level = (u1, u2, u3)[t]
        delta = (d1, d2, d3)[t]
        delta_before = (None, d1, d2)[t]
        delta_next = (d2, d3, e4)[t]

        def body(j):
            values = []
            for p in pair:
                prior = None if delta_before is None else inner(delta_before.at[p])
                step = advance(delta.at[p], prior, j)
                for i, c in enumerate(cols):
                    step[i] = step[i] + vec[p, j, :, c] * level[j + 1, :, c]
                    if t == 2:
                        step[i] = weight[j, :, c] * step[i]
                    delta_next[p, j + 1, :, c] = step[i]
                values.append(step)
            if t == 2:
                for i, c in enumerate(cols):
                    total[j, :, c] = total[j, :, c] + level[j + 1, :, c] * chosen(j, values, i)

        sweep(body)
        for p in pair:
            halo(delta_next.at[p])

    def adjoint(m, t):
        field = (e4, e3, e2)[t]
        before = (None, e4, e3)[t]
        result = (e3, e2, None)[t]
        delta = (d3, d2, d1)[t]
        level = (u2, u1, lev.at[m, 1])[t]

        def body(j):
            values = []
            for p in pair:
                prior = None if before is None else inner(before.at[p])
                step = advance(field.at[p], prior, j)
                for i, c in enumerate(cols):
                    step[i] = step[i] + weight[j, :, c] * delta[p, j + 1, :, c]
                    if result is not None:
                        result[p, j + 1, :, c] = step[i]
                values.append(step)
            for i, c in enumerate(cols):
                total[j, :, c] = total[j, :, c] + level[j + 1, :, c] * chosen(j, values, i)

        if result is None:
            for k in range(num_shot_devices):
                sweep(body, k * part_tiles, (k + 1) * part_tiles)
                pl.when(m == members - 1)(lambda k=k: start_swap(k))
        else:
            sweep(body)
        if result is not None:
            for p in pair:
                halo(result.at[p])

    def piece(k, device):
        first = pl.multiple_of(device * share, share)
        return total.at[pl.ds(k * part_tiles, part_tiles), pl.ds(first, share), :]

    def start_swap(k):
        for away in range(1, num_shot_devices):
            other = (shot + away) % num_shot_devices
            pltpu.make_async_remote_copy(
                src_ref=piece(k, other),
                dst_ref=partial.at[away - 1, :, pl.ds(k * share, share), :],
                send_sem=swap_send.at[0],
                recv_sem=swap_recv.at[away - 1],
                device_id={"shot": other},
                device_id_type=MESH,
            ).start()
        pltpu.make_async_copy(
            piece(k, shot), packed.at[:, pl.ds(k * share, share), :], pack_sem.at[0]
        ).start()

    def combine(j):
        at = pl.ds(j, block)
        value = packed[at]
        for away in range(1, num_shot_devices):
            value = value + partial[away - 1, at]
        value = tiled(shuffle(flat(value), collect_table)) * inverse[at]
        for p in pair:
            for i in range(block):
                keep = parity_out[j + i] != p % 2
                for n, c in enumerate(cols):
                    piece_of = value[i, :, n * LANE : (n + 1) * LANE] - coarse_in[p, j + i, :, c]
                    result_out[p, j + i, :, c] = jnp.where(keep, piece_of, 0.0)

    def deliver(j):
        for p in pair:
            for k in range(num_shot_devices):
                for e in range(share):
                    first = e * tiles + k * part_tiles + j
                    pltpu.make_async_copy(
                        result_out.at[p, pl.ds(j, block), k * share + e, :],
                        out_hbm.at[p, pl.ds(first, block), :],
                        out_sem.at[0],
                    ).start()

    work = []

    def add_work(run, ref=None, sem=None):
        def first():
            if ref is not None:
                await_bytes(ref, sem)
            run(0)

        work.append(first)
        for b in range(1, tiles // block):
            work.append(lambda b=b: run(b * block))

    def clear_total():
        total[...] = jnp.zeros_like(total)

    work.append(clear_total)
    work.append(prepare_sources)
    add_work(prepare_coefficient, coefficient_in, load_sem.at[0])
    add_work(prepare_weight, receiver_in, load_sem.at[1])
    add_work(prepare_vectors, probes_in, load_sem.at[2])

    def out_work():
        await_bytes(inverse, load_sem.at[3])
        prepare_out()
        await_bytes(coarse_in, load_sem.at[4])

    work.insert(1, out_work)
    def gather_plan():
        last = members - 1
        plan = [lambda: column(0, 1), lambda: relay(last, 0), lambda: relay(0, 0)]
        for k in range(2, line):
            plan += [lambda k=k: column(0, k), lambda k=k: column(last, k - 1)]
            plan += [lambda k=k: relay(0, k - 1), lambda k=k: across(last, k - 2)]
        plan += [lambda: relay(0, line - 1), lambda: column(last, line - 1)]
        return plan, [lambda: across(last, line - 1)]

    before, after = gather_plan()
    while len(work) > len(before):
        work.pop(0)()
    for step in before:
        step()
        if work:
            work.pop(0)()
    for rest in work:
        rest()
    def arrived(m):
        if m == members - 1:
            for step in after:
                step()
            line_sends_end()
        gather_end(m)
        if m == 0:
            across(members - 1, line - 2)

    def member(m, carry):
        for i in range(members):
            pl.when(m == i)(lambda i=i: arrived(i))
        start_fields(m)
        for t in range(3):
            levels_step(m, t)
        for t in range(3):
            forward(m, t)
        for t in range(3):
            adjoint(m, t)
        return carry

    lax.fori_loop(0, members, member, 0)
    await_bytes(packed, pack_sem.at[0])
    for away in range(1, num_shot_devices):
        await_bytes(partial.at[away - 1], swap_recv.at[away - 1])
    for b in range(part_tiles // block):
        combine(b * block)
        deliver(b * block)
    await_bytes(partial, swap_send.at[0])
    await_bytes(counter, send_sem.at[0])
    await_bytes(result_out, out_sem.at[0])


def on_device(
    num_shot_devices,
    num_probe_devices,
    probes,
    coarse_sample,
    coefficient,
    receiver,
    checkpoints,
    encodings,
    wavelet,
    bounds,
):
    members, levels, chunk, width = checkpoints.shape
    num_probes, num_rows, _ = probes.shape
    out_rows = coarse_sample.shape[1]
    tiles = num_rows // SUB
    line = num_probe_devices // INNER
    f32 = jnp.float32

    part_tiles = tiles // num_shot_devices
    whole_pieces = members * 3 * line - (line - 1)

    def plain(*lead):
        return pltpu.VMEM((*lead, tiles, SUB, width), f32)

    def ringed(*lead):
        return pltpu.VMEM((*lead, tiles + 2, SUB, width), f32)

    def part(*lead):
        return pltpu.VMEM((*lead, part_tiles, SUB, width), f32)

    others = num_shot_devices - 1
    anywhere = pl.BlockSpec(memory_space=pl.ANY)
    vmem = pl.BlockSpec(memory_space=pltpu.VMEM)
    return pl.pallas_call(
        functools.partial(kernel, num_shot_devices, num_probe_devices),
        out_shape=jax.ShapeDtypeStruct(coarse_sample.shape, f32),
        in_specs=[pl.BlockSpec(memory_space=pltpu.SMEM), vmem, vmem] + [anywhere] * 5,
        out_specs=anywhere,
        scratch_shapes=[
            pltpu.VMEM(checkpoints.shape, f32),
            pltpu.VMEM(checkpoints.shape, f32),
            plain(num_probes),
            part(num_probes),
            plain(),
            plain(),
            part(),
            pltpu.VMEM((width, width), jnp.bfloat16),
            pltpu.VMEM((width, width), jnp.bfloat16),
            pltpu.VMEM((tiles, SUB, LANE), jnp.int32),
            pltpu.VMEM((part_tiles, SUB, LANE), jnp.int32),
            plain(),
            plain(),
            plain(),
            plain(num_probes + 1),
            ringed(members, levels),
            pltpu.VMEM((whole_pieces, levels, chunk, width), f32),
            ringed(),
            ringed(),
            ringed(),
            ringed(num_probes),
            ringed(num_probes),
            ringed(num_probes),
            ringed(num_probes),
            ringed(num_probes),
            ringed(num_probes),
            plain(),
            part(),
            part(others),
            part(num_probes),
            pltpu.VMEM((members, SUB, width), f32),
            pltpu.SemaphoreType.DMA((5,)),
            pltpu.SemaphoreType.DMA((1 + members,)),
            pltpu.SemaphoreType.DMA((members, 4, line, levels)),
            pltpu.SemaphoreType.DMA((members,)),
            pltpu.SemaphoreType.DMA((2,)),
            pltpu.SemaphoreType.DMA((1,)),
            pltpu.SemaphoreType.DMA((1,)),
            pltpu.SemaphoreType.DMA((1,)),
            pltpu.SemaphoreType.DMA((others,)),
        ],
        compiler_params=pltpu.CompilerParams(
            collective_id=0, has_side_effects=True, vmem_limit_bytes=60 * 1024 * 1024
        ),
    )(
        bounds,
        encodings,
        wavelet,
        probes,
        coarse_sample,
        coefficient,
        receiver,
        checkpoints,
    )


def solution(mesh):
    return jax.shard_map(
        functools.partial(on_device, mesh.shape["shot"], mesh.shape["probe"]),
        mesh=mesh,
        in_specs=(
            P("probe", None, None),
            P("probe", "shot", None),
            P(),
            P(),
            P("shot", None, "probe", None),
            P("shot", None),
            P(),
            P(),
        ),
        out_specs=P("probe", "shot", None),
        check_vma=False,
    )
```
